32 devices in a mesh: groups: 2 (over y), ctx: 4 (over z), tp: 4 (over x, core).
Axes of the slice: x: 2, y: 2, z: 4, core: 2. Of those that a mesh axis runs over, the one named last changes fastest.
Arguments:
- streams: bfloat16 [3, 1024, 8192], P(None, ('groups', 'ctx'), 'tp'), parts along dimension 1, may hold values from -6 to 6
- short_filter: float32 [3, 3, 8192], P(None, None, 'tp'), may hold values from -3 to 3
- decay_rate: float32 [8192, 16], P('tp'), may hold values from 0 to 1
- residue: float32 [8192, 16], P('tp'), may hold values from -0.2 to 0.2
- skip_gain: float32 [8192], P('tp'), may hold values from -4 to 4
- lengths: int32 [4], P('groups'), parts along dimension 0, may hold values from 1 to 448, 512 in all
- queries: bfloat16 [1024, 8192], P(('groups', 'ctx'), 'tp'), parts along dimension 0, may hold values from -8 to 8
- keys: bfloat16 [1024, 8192], P(('groups', 'ctx'), 'tp'), parts along dimension 0, may hold values from -8 to 8
Outputs:
- hyena_out: bfloat16 [1024, 8192], P(('groups', 'ctx'), 'tp'), parts along dimension 0
- attended: bfloat16 [1024, 8192], P(('groups', 'ctx'), 'tp'), parts along dimension 0
The draws below stay inside these ranges and needn't reach their ends.
There are 2 independent parts, one for each index of `groups`. The reference program is written for one: setup_inputs(seed, part) draws one part's arguments, and reference() takes and returns one part's arrays. A program takes and returns all parts, laid end to end along the dimension named above; an argument that names none is the same for every part. Nothing has to cross between parts.
Inputs may be any that keep to these rules, and one draw needn't show every extreme that they name: The requests fill the group in order, their lengths sum to 512, and the longest has at most 448 tokens.
All inputs are finite; a program needn't handle non-finite values.
Results may differ from the reference program's by a relative error of at most 0.01.
Values may be sent and summed in bfloat16 or wider, within the bound.
No kernel may reach another device: no remote copies, remote signals or barrier semaphores. Data moves between devices by JAX's collectives and lax.ppermute only.
A program may use at most 128 MiB of HBM per device.

```python
import math
import jax
import jax.numpy as jnp
import numpy as np
from jax import lax

D = 8192
HEADS = 64
HEAD_DIM = 128
MODES = 16
SHORT = 3
REQS = 2
TOKENS = 512
MOST = 448


def draw_decay_rate(key, part):
    shape = (D, MODES)
    first_key = jax.random.fold_in(key, 11)
    return jnp.exp(jax.random.uniform(first_key, shape, jnp.float32, math.log(0.5 / TOKENS), math.log(1.0 / 30.0))).astype(jnp.float32)


def base_field(key, salt):
    field_key = jax.random.fold_in(key, salt)
    return jnp.clip(jax.random.normal(field_key, (TOKENS, D), jnp.float32), -6.0, 6.0)


def draw_queries(key, part):
    field = base_field(key, 1)
    return field.astype(jnp.bfloat16)


def draw_keys(key, part):
    field = base_field(key, 2)
    return field.astype(jnp.bfloat16)


def shard_levels(key, dims, shards, least, top_value):
    def one(position, blocks):
        heights = jax.random.uniform(jax.random.fold_in(jax.random.fold_in(key, 6), position), (blocks,), jnp.float32, least / len(shards), top_value / len(shards))
        return jnp.repeat(jnp.exp(heights), dims[position] // blocks).reshape((-1,) + (1,) * (len(dims) - position - 1))

    loudness = one(*shards[0])
    for cut in shards[1:]:
        loudness = loudness * one(*cut)
    return loudness


def length_profile(count, total, bound, slope):
    loads = [(1 << 20) // math.isqrt(standing ** slope) + 1 for standing in range(2, count + 1)]
    spare, given = total - bound - (count - 1), [1] * (count - 1)
    while spare > 0:
        movable = [i for i in range(count - 1) if given[i] < bound]
        whole, budget = sum([loads[i] for i in movable]), spare
        for i in movable:
            more = min(bound - given[i], max(1, budget * loads[i] // whole), spare)
            given[i] = given[i] + more
            spare = spare - more
    return np.array([bound] + given)


def ragged(stream_key, count, total, limit, lean):
    if count == 2:
        one = jax.random.randint(stream_key, (), max(1, total - limit), min(limit, total - 1) + 1)
        return jnp.stack([one, total - one])
    sizes = jnp.asarray(length_profile(count, total, limit, lean), jnp.int32)
    couples = (count - 1) // 2
    giver, taker = sizes[1:1 + 2 * couples:2], sizes[2:2 + 2 * couples:2]
    margin = jnp.minimum(giver - 1, limit - taker)
    moved = jax.random.randint(jax.random.fold_in(stream_key, 1), (couples,), 0, 1 << 20) % (margin + 1)
    sizes = sizes.at[1:1 + 2 * couples:2].set(giver - moved).at[2:2 + 2 * couples:2].set(taker + moved)
    return sizes[jax.random.permutation(jax.random.fold_in(stream_key, 2), count)]


def gaussian(stream_key, shape, scale, reach, split=(), kind=jnp.bfloat16):
    result = scale * jax.random.normal(stream_key, shape, jnp.float32)
    if split:
        result = result * shard_levels(stream_key, shape, split, -0.22, 0.18)
    return jnp.clip(result, -reach, reach).astype(kind)


def setup_inputs(seed: int = 0, part: int = 0) -> dict:
    splits = jax.random.split(jax.random.key(seed), 9)
    part_splits = jax.random.split(jax.random.fold_in(splits[8], part), 9)
    return {
        "streams": gaussian(part_splits[0], (3, TOKENS, D), 1.0, 6.0, ((1, 4), (2, 4))),
        "short_filter": gaussian(splits[1], (SHORT, 3, D), 0.6, 3.0, ((2, 4),), jnp.float32),
        "decay_rate": draw_decay_rate(jax.random.fold_in(splits[8], 71), part),
        "residue": gaussian(splits[3], (D, MODES), 0.03, 0.2, ((0, 4),), jnp.float32),
        "skip_gain": gaussian(splits[4], (D,), 1.0, 4.0, ((0, 4),), jnp.float32),
        "lengths": ragged(part_splits[5], REQS, TOKENS, MOST, 2).astype(jnp.int32),
        "queries": draw_queries(jax.random.fold_in(jax.random.fold_in(splits[8], part), 71), part),
        "keys": draw_keys(jax.random.fold_in(jax.random.fold_in(splits[8], part), 71), part),
    }


def documents(lengths):
    ends = jnp.cumsum(lengths).astype(jnp.int32)
    places = jnp.arange(TOKENS, dtype=jnp.int32)
    return lax.optimization_barrier(jnp.sum((places[:, None] >= ends[None, :]).astype(jnp.int32), axis=1)).astype(jnp.int32)

def reference(streams, short_filter, decay_rate, residue, skip_gain, lengths, queries, keys):
    document = documents(lengths)
    data = streams.astype(jnp.float32)
    filtered = jnp.zeros(data.shape, jnp.float32)
    for tap in range(SHORT):
        shifted = jnp.pad(data, ((0, 0), (tap, 0), (0, 0)))[:, :TOKENS, :]
        doc_shift = jnp.pad(document, (tap, 0), constant_values=-1)[:TOKENS]
        same = (doc_shift == document).astype(jnp.float32)
        filtered = filtered + short_filter[tap][:, None, :] * shifted * same[None, :, None]
    mixed = filtered[1] * filtered[2]
    decay = jnp.exp(-decay_rate)
    linked = jnp.concatenate([jnp.zeros((1,), jnp.float32), (document[1:] == document[:-1]).astype(jnp.float32)])

    def advance(state, inputs):
        row, flag = inputs
        state = state * decay * flag + row[:, None]
        return (state, lax.optimization_barrier(jnp.sum(residue * state, axis=1)))
    _, long = lax.scan(advance, jnp.zeros((D, MODES), jnp.float32), (mixed, linked))
    long = long + skip_gain[None, :] * mixed
    hyena_out = (filtered[0] * long).astype(jnp.bfloat16)
    scale = 1.0 / math.sqrt(HEAD_DIM)
    places = jnp.arange(TOKENS, dtype=jnp.int32)
    allowed = (places[None, :] <= places[:, None]) & (document[None, :] == document[:, None])
    query_heads = queries.reshape(TOKENS, HEADS, HEAD_DIM).transpose(1, 0, 2)
    key_heads = keys.reshape(TOKENS, HEADS, HEAD_DIM).transpose(1, 0, 2)
    value_heads = hyena_out.reshape(TOKENS, HEADS, HEAD_DIM).transpose(1, 0, 2)

    def one_head(items):
        query, key, value = items
        scores = jnp.dot(query.astype(jnp.float32), key.astype(jnp.float32).T, precision=lax.Precision.HIGHEST) * scale
        top = lax.optimization_barrier(jnp.max(jnp.where(allowed, scores, -jnp.inf), axis=1))
        weight = jnp.where(allowed, jnp.exp(scores - top[:, None]), 0.0)
        total = lax.optimization_barrier(jnp.sum(weight, axis=1))
        weight_low = lax.optimization_barrier(weight.astype(jnp.bfloat16)).astype(jnp.float32)
        summed = jnp.dot(weight_low, value.astype(jnp.float32), precision=lax.Precision.HIGHEST)
        return summed / total[:, None]
    heads_out = lax.map(one_head, (query_heads, key_heads, value_heads))
    attended = heads_out.transpose(1, 0, 2).reshape(TOKENS, D).astype(jnp.bfloat16)
    return (hyena_out, attended)
```

```python
import functools
import math

import jax
import jax.numpy as jnp
from jax import lax
from jax.experimental import pallas as pl
from jax.experimental.pallas import tpu as pltpu
from jax.sharding import PartitionSpec as P

HEAD_DIM = 128
SHORT = 3
LANES = 128
NEG = -1e30


SMEM = pl.BlockSpec(memory_space=pltpu.SMEM)
VMEM = pl.BlockSpec(memory_space=pltpu.VMEM)


def ends_of(lengths_ref):
    ends, total = [], jnp.int32(0)
    for r in range(lengths_ref.shape[0]):
        total = total + lengths_ref[r]
        ends.append(total)
    return ends


def start_of(place, ends):
    start = jnp.zeros_like(place)
    for end in ends:
        start = jnp.where(place >= end, end, start)
    return start


def end_of(place, ends):
    stop = ends[-1]
    for end in reversed(ends):
        stop = jnp.where(place < end, end, stop)
    return stop


def call(body, out, n_in, n_smem=1, scratch=(), name=None, flops=10**7, moved=4 * 10**6):
    return pl.pallas_call(
        body,
        out_shape=out,
        in_specs=[SMEM] * n_smem + [VMEM] * (n_in - n_smem),
        out_specs=jax.tree.map(lambda _: VMEM, out),
        scratch_shapes=list(scratch),
        compiler_params=pltpu.CompilerParams(vmem_limit_bytes=40 << 20),
        cost_estimate=pl.CostEstimate(flops=flops, bytes_accessed=moved, transcendentals=0),
        name=name,
    )


def hyena_local(lengths_ref, streams_ref, rim_ref, taps_ref, decay_ref, residue_ref, skip_ref,
                gate_ref, long_ref, state_ref, step_ref, block_ref, low_ref, high_ref,
                mixed_ref, gain_ref, final_ref):
    rows, width = gate_ref.shape
    modes = decay_ref.shape[1]
    tiles = width // LANES
    half = width // 2
    index = lax.axis_index("ctx")
    first = index * rows
    ends = ends_of(lengths_ref)

    row = lax.broadcasted_iota(jnp.int32, (rows, LANES), 0)
    place = row + first
    start = start_of(place, ends)
    inside = [None] + [(place - i >= start).astype(jnp.float32) for i in range(1, SHORT)]

    for j in range(tiles):
        lanes = slice(j * LANES, (j + 1) * LANES)
        filtered = []
        for s in range(3):
            x = streams_ref[s, :, lanes].astype(jnp.float32)
            rim = rim_ref[s, :, lanes].astype(jnp.float32)
            total = taps_ref[0, s : s + 1, lanes] * x
            for i in range(1, SHORT):
                moved = pltpu.roll(x, i, 0)
                for k in range(i):
                    moved = jnp.where(row == k, rim[SHORT - 1 - i + k : SHORT - i + k, :], moved)
                total = total + taps_ref[i, s : s + 1, lanes] * moved * inside[i]
            filtered.append(total)
        gate_ref[:, lanes] = filtered[0]
        mixed_ref[pl.ds(j, rows, stride=tiles), :] = filtered[1] * filtered[2]
        rate = decay_ref[j * LANES : (j + 1) * LANES, :].T
        step_ref[pl.ds(j, modes, stride=tiles), :] = jnp.exp(-rate)
        block_ref[pl.ds(j, modes, stride=tiles), :] = jnp.exp(-rate * rows)
        gain_ref[pl.ds(j, modes, stride=tiles), :] = residue_ref[j * LANES : (j + 1) * LANES, :].T

    for h in range(tiles // 8):
        decay = [step_ref[m * tiles + h * 8 : m * tiles + h * 8 + 8, :] for m in range(modes)]
        gain = [gain_ref[m * tiles + h * 8 : m * tiles + h * 8 + 8, :] for m in range(modes)]
        skip = skip_ref[h * 8 : h * 8 + 8, :]

        def advance(t, state):
            at = pl.ds(pl.multiple_of(t * tiles + h * 8, 8), 8)
            x = mixed_ref[at, :]
            state = tuple(s * d + g * x for s, d, g in zip(state, decay, gain))
            terms = list(state) + [skip * x]
            while len(terms) > 1:
                terms = [a + b for a, b in zip(terms[::2], terms[1::2])] + (
                    [terms[-1]] if len(terms) % 2 else []
                )
            long_ref[at, :] = terms[0]
            return state

        low = jnp.int32(0)
        for end in ends:
            high = jnp.clip(end - first, 0, rows)
            low_row = low

            def four(g, state, low_row=low_row):
                for u in range(4):
                    state = advance(low_row + g * 4 + u, state)
                return state

            groups = lax.shift_right_logical(high - low_row, 2)
            state = tuple(jnp.zeros((8, LANES), jnp.float32) for _ in range(modes))
            state = lax.fori_loop(0, groups, four, state)
            state = lax.fori_loop(low_row + groups * 4, high, advance, state)

            @pl.when((low_row < high) & (high == rows))
            def _(state=state):
                for m in range(modes):
                    final_ref[m * tiles + h * 8 : m * tiles + h * 8 + 8, :] = state[m]

            low = high
    state_ref[...] = final_ref[...].astype(state_ref.dtype)

    @pl.when(index == 0)
    def _():
        for j in range(tiles):
            lanes = slice(j * LANES, (j + 1) * LANES)
            value = gate_ref[:, lanes] * long_ref[pl.ds(j, rows, stride=tiles), :]
            out, at = (low_ref, j) if j * LANES < half else (high_ref, j - tiles // 2)
            out[:, at * LANES : (at + 1) * LANES] = value.astype(out.dtype)


def hyena_cross(hops, lengths_ref, step_ref, block_ref, long_ref, gate_ref, *refs):
    parts = refs[: len(hops)]
    value_ref, send_ref, cross_ref = refs[len(hops) :]
    rows, width = gate_ref.shape
    tiles = width // LANES
    modes = step_ref.shape[0] // tiles
    half = width // 2
    index = lax.axis_index("ctx")
    first = index * rows
    ends = ends_of(lengths_ref)
    start = start_of(first - 1, ends)
    count = jnp.where(index > 0, jnp.clip(end_of(first - 1, ends) - first, 0, rows), 0)
    keeps = [
        ((first - 1 - hop * rows >= start) & (index > hop)).astype(jnp.float32) for hop in hops
    ]

    @pl.when(count > 0)
    def _():
        for h in range(tiles // 8):
            decay, incoming = [], []
            for m in range(modes):
                at = slice(m * tiles + h * 8, m * tiles + h * 8 + 8)
                decay.append(step_ref[at, :])
                total, factor = None, None
                for hop, keep, part in zip(hops, keeps, parts):
                    term = part[at, :].astype(jnp.float32) * keep
                    if hop:
                        factor = block_ref[at, :] if factor is None else factor * block_ref[at, :]
                        term = term * factor
                    total = term if total is None else total + term
                incoming.append(total)

            def advance(t, state):
                at = pl.ds(pl.multiple_of(t * tiles + h * 8, 8), 8)
                state = tuple(s * d for s, d in zip(state, decay))
                terms = list(state)
                while len(terms) > 1:
                    terms = [a + b for a, b in zip(terms[::2], terms[1::2])] + (
                        [terms[-1]] if len(terms) % 2 else []
                    )
                cross_ref[at, :] = terms[0]
                return state

            def four(g, state):
                for u in range(4):
                    state = advance(g * 4 + u, state)
                return state

            groups = lax.shift_right_logical(count, 2)
            state = lax.fori_loop(0, groups, four, tuple(incoming))
            lax.fori_loop(groups * 4, count, advance, state)

    row = lax.broadcasted_iota(jnp.int32, (rows, LANES), 0)
    reached = row < count
    for j in range(tiles):
        lanes = slice(j * LANES, (j + 1) * LANES)
        every = pl.ds(j, rows, stride=tiles)
        long = long_ref[every, :] + jnp.where(reached, cross_ref[every, :], 0.0)
        value_ref[:, lanes] = (gate_ref[:, lanes] * long).astype(value_ref.dtype)

    if send_ref.shape[1] == half:
        copy_half(value_ref, send_ref, index % 2 == 1)


def copy_half(source_ref, target_ref, lower):
    half = target_ref.shape[1]

    @pl.when(lower)
    def _():
        target_ref[...] = source_ref[:, :half]

    @pl.when(jnp.logical_not(lower))
    def _():
        target_ref[...] = source_ref[:, half:]


def pack(streams_ref, queries_ref, keys_ref, rim_ref, q_near, q_far, k_near, k_far):
    reach_back = SHORT - 1
    last = streams_ref.shape[1]
    half = q_far.shape[1]
    odd = lax.axis_index("ctx") % 2 == 1
    rim_ref[...] = streams_ref[:, last - reach_back :, :]
    copy_half(queries_ref, q_near, odd)
    copy_half(keys_ref, k_near, odd)
    q_far[...] = queries_ref[:, half:]
    k_far[...] = keys_ref[:, :half]


def biases(query_block, key_blocks, rows, ends):
    place = query_block * rows + lax.broadcasted_iota(jnp.int32, (rows, rows), 0)
    start = start_of(place, ends)
    out = []
    for block in key_blocks:
        key = block * rows + lax.broadcasted_iota(jnp.int32, (rows, rows), 1)
        out.append(jnp.where((key >= start) & (key <= place), 0.0, NEG))
    return out


def one_head(query, pairs, bias):
    scale = 1.0 / math.sqrt(HEAD_DIM)
    dims = (((1,), (1,)), ((), ()))
    scores = [
        lax.dot_general(query, key(), dims, preferred_element_type=jnp.float32) * scale + b
        for (key, _), b in zip(pairs, bias)
    ]
    top = scores[0]
    for s in scores[1:]:
        top = jnp.maximum(top, s)
    top = jnp.max(top, axis=1, keepdims=True)
    weights = [jnp.exp(s - top) for s in scores]
    total = weights[0]
    for w in weights[1:]:
        total = total + w
    total = jnp.sum(total, axis=1, keepdims=True)
    summed = None
    for w, (_, value) in zip(weights, pairs):
        part = jnp.dot(w.astype(jnp.bfloat16), value(), preferred_element_type=jnp.float32)
        summed = part if summed is None else summed + part
    return summed / total, top + jnp.log(total)


def heads(out, query_of, pairs_of, bias, count):
    for h in range(count):
        out(h, *one_head(query_of(h), pairs_of(h), bias))


def cut(ref, h):
    return ref[:, h * HEAD_DIM : (h + 1) * HEAD_DIM]


def split3(x):
    a = x.astype(jnp.bfloat16)
    rest = x - a.astype(jnp.float32)
    b = rest.astype(jnp.bfloat16)
    c = (rest - b.astype(jnp.float32)).astype(jnp.bfloat16)
    return a, b, c


def hub(lengths_ref, q1_ref, q2_ref, key_ref, value_ref, k1_ref, va_ref, vb_ref, k2_ref, v2_ref,
        near_ref, far_ref):
    rows, half = q1_ref.shape
    count = half // HEAD_DIM
    index = lax.axis_index("ctx")
    ends = ends_of(lengths_ref)
    lane = lax.broadcasted_iota(jnp.int32, (rows, LANES), 1)

    def run(q_ref, out_ref, ahead, offset, sources):
        bias = biases(index + ahead, [index - back for back, _, _ in sources], rows, ends)
        stats = jnp.zeros((rows, LANES), jnp.float32)
        for h in range(count):
            pairs = [
                (functools.partial(cut, k, h + o), functools.partial(cut, v, h + o))
                for (_, k, v), o in zip(sources, [offset] + [0] * (len(sources) - 1))
            ]
            mean, log_total = one_head(cut(q_ref, h), pairs, bias)
            out_ref[:, h * HEAD_DIM : (h + 1) * HEAD_DIM] = mean.astype(out_ref.dtype)
            for part, piece in enumerate(split3(log_total)):
                stats = jnp.where(lane == 3 * h + part, piece.astype(jnp.float32), stats)
        out_ref[:, half:] = stats.astype(out_ref.dtype)

    @pl.when(index == 0)
    def _():
        run(q1_ref, near_ref, 1, 0, [(0, key_ref, value_ref)])

    @pl.when(index == 1)
    def _():
        sources = [(0, key_ref, value_ref), (1, k1_ref, va_ref)]
        run(q2_ref, far_ref, 2, count, sources)
        run(q1_ref, near_ref, 1, count, sources)

    @pl.when(index == 2)
    def _():
        run(q1_ref, near_ref, 1, 0,
            [(0, key_ref, value_ref), (1, k1_ref, vb_ref), (2, k2_ref, v2_ref)])


def own(lengths_ref, query_ref, key_ref, value_ref, k1_ref, va_ref, vb_ref, k2_ref, v2_ref,
        mean_ref, stat_ref):
    rows, width = query_ref.shape
    half = width // 2
    count = half // HEAD_DIM
    index = lax.axis_index("ctx")
    ends = ends_of(lengths_ref)
    lane = lax.broadcasted_iota(jnp.int32, (rows, LANES), 1)

    def run(base, sources):
        bias = biases(index, [index - back for back, _, _ in sources], rows, ends)
        stats = jnp.zeros((rows, LANES), jnp.float32) if base == 0 else stat_ref[...]
        for h in range(count):
            pairs = [
                (functools.partial(cut, k, h + o), functools.partial(cut, v, h + o))
                for (_, k, v), o in zip(sources, [base] + [0] * (len(sources) - 1))
            ]
            mean, log_total = one_head(cut(query_ref, h + base), pairs, bias)
            mean_ref[:, (h + base) * HEAD_DIM : (h + base + 1) * HEAD_DIM] = mean
            stats = jnp.where(lane == h + base, log_total, stats)
        stat_ref[...] = stats

    here = (0, key_ref, value_ref)

    @pl.when(index == 2)
    def _():
        run(0, [here, (1, k1_ref, vb_ref), (2, k2_ref, v2_ref)])

    @pl.when(index != 2)
    def _():
        run(0, [here])

    @pl.when(index == 1)
    def _():
        run(count, [here, (1, k1_ref, va_ref)])

    @pl.when(index == 3)
    def _():
        run(count, [here, (1, k1_ref, vb_ref)])

    @pl.when(index % 2 == 0)
    def _():
        run(count, [here])


def merge(mean_ref, stat_ref, near_ref, far_ref, out_ref):
    rows, width = mean_ref.shape
    half = width // 2
    count = half // HEAD_DIM
    index = lax.axis_index("ctx")

    def join(base, other_ref):
        for h in range(count):
            at = slice((h + base) * HEAD_DIM, (h + base + 1) * HEAD_DIM)
            here = stat_ref[:, h + base : h + base + 1]
            there = sum(
                other_ref[:, half + 3 * h + k : half + 3 * h + k + 1].astype(jnp.float32)
                for k in range(3)
            )
            top = jnp.maximum(here, there)
            a, b = jnp.exp(here - top), jnp.exp(there - top)
            norm = 1.0 / (a + b)
            other = other_ref[:, h * HEAD_DIM : (h + 1) * HEAD_DIM].astype(jnp.float32)
            out_ref[:, at] = (mean_ref[:, at] * (a * norm) + other * (b * norm)).astype(out_ref.dtype)

    def keep(base):
        at = slice(base * HEAD_DIM, (base + count) * HEAD_DIM)
        out_ref[:, at] = mean_ref[:, at].astype(out_ref.dtype)

    @pl.when(index % 2 == 1)
    def _():
        join(0, near_ref)

    @pl.when(index % 2 == 0)
    def _():
        keep(0)

    @pl.when(index < 2)
    def _():
        keep(count)

    @pl.when(index == 2)
    def _():
        join(count, near_ref)

    @pl.when(index == 3)
    def _():
        join(count, far_ref)


def doc_of(places, ends):
    return jnp.sum((places[:, None] >= ends[None, :]).astype(jnp.int32), axis=1)


def gathered_attention(lengths, queries, keys, values):
    rows, width = queries.shape
    heads_here = width // HEAD_DIM
    ends = jnp.cumsum(lengths)
    places = lax.axis_index("ctx") * rows + jnp.arange(rows, dtype=jnp.int32)
    piece = lax.all_gather(jnp.stack([keys, values]), "ctx", axis=1, tiled=True)
    count = piece.shape[1]
    key_places = jnp.arange(count, dtype=jnp.int32)
    allowed = (key_places[None, :] <= places[:, None]) & (
        doc_of(key_places, ends)[None, :] == doc_of(places, ends)[:, None]
    )
    scores = jnp.einsum(
        "qhd,khd->hqk",
        queries.reshape(rows, heads_here, HEAD_DIM),
        piece[0].reshape(count, heads_here, HEAD_DIM),
        preferred_element_type=jnp.float32,
    )
    masked = jnp.where(allowed[None], scores * (1.0 / math.sqrt(HEAD_DIM)), NEG)
    weight = jnp.exp(masked - jnp.max(masked, axis=2, keepdims=True))
    total = jnp.sum(weight, axis=2)
    summed = jnp.einsum(
        "hqk,khd->hqd",
        weight.astype(jnp.bfloat16),
        piece[1].reshape(count, heads_here, HEAD_DIM),
        preferred_element_type=jnp.float32,
    )
    return (summed / total[..., None]).transpose(1, 0, 2).reshape(rows, width).astype(jnp.bfloat16)


def send(value, pairs):
    return lax.ppermute(value, "ctx", pairs)


def shift(value, steps):
    count = lax.axis_size("ctx")
    return send(value, [(i, i + steps) for i in range(count) if 0 <= i + steps < count])


def shards(streams, short_filter, decay_rate, residue, skip_gain, lengths, queries, keys):
    f32, bf16 = jnp.float32, jnp.bfloat16
    shape = jax.ShapeDtypeStruct
    rows, width = streams.shape[1:]
    half = width // 2
    modes = decay_rate.shape[1]
    tiles = width // LANES
    ctx = lax.axis_size("ctx")
    paired = ctx == 4 and (width // HEAD_DIM) % 2 == 0

    if paired:
        halves = shape((rows, half), bf16)
        rim, q_near, q_far, k_near, k_far = call(
            pack, (shape((3, SHORT - 1, width), bf16), halves, halves, halves, halves), 3, 0,
            name="pack",
        )(streams, queries, keys)
        rim = shift(rim, 1)
        q1 = shift(q_near, -1)
        q2 = send(q_far, [(3, 1)])
        k1 = shift(k_near, 1)
        k2 = send(k_far, [(0, 2)])
    else:
        rim = shift(streams[:, rows - SHORT + 1 :, :], 1)

    states = (modes * tiles, LANES)
    gate, long, state, step, block, low, high = call(
        hyena_local,
        (
            shape((rows, width), f32),
            shape((rows * tiles, LANES), f32),
            shape(states, bf16),
            shape(states, f32),
            shape(states, f32),
            shape((rows, half), bf16),
            shape((rows, half), bf16),
        ),
        7,
        scratch=[
            pltpu.VMEM((rows * tiles, LANES), f32),
            pltpu.VMEM(states, f32),
            pltpu.VMEM(states, f32),
        ],
        name="hyena_local",
    )(lengths, streams, rim, short_filter, decay_rate, residue, skip_gain.reshape(tiles, LANES))

    if paired:
        va = send(high, [(0, 1)])
        v2 = send(low, [(0, 2)])
        parts = [shift(state, hop + 1) for hop in range(ctx - 1)]
        hops = tuple(range(ctx - 1))
    else:
        every = lax.all_gather(state, "ctx").astype(f32)
        ends = jnp.cumsum(lengths)
        before = lax.axis_index("ctx") * rows - 1
        lasts = (jnp.arange(ctx, dtype=jnp.int32) + 1) * rows - 1
        same = (lasts <= before) & (
            doc_of(lasts, ends) == doc_of(jnp.reshape(before, (1,)), ends)
        )
        factor = jnp.where(same, (before - lasts) // rows, 0).astype(f32)
        weight = same.astype(f32)[:, None, None] * block[None] ** factor[:, None, None]
        parts = [jnp.sum(weight * every, axis=0)]
        hops = (0,)

    value, value_near = call(
        functools.partial(hyena_cross, hops),
        (shape((rows, width), bf16), shape((rows, half if paired else width), bf16)),
        5 + len(hops),
        scratch=[pltpu.VMEM((rows * tiles, LANES), f32)],
        name="hyena_cross",
    )(lengths, step, block, long, gate, *parts)

    if not paired:
        return value, gathered_attention(lengths, queries, keys, value)

    vb = send(value_near, [(1, 2), (2, 3)])
    wide = shape((rows, half + LANES), bf16)
    o_near, o_far = call(hub, (wide, wide), 10, name="hub")(
        lengths, q1, q2, keys, value, k1, va, vb, k2, v2
    )
    far = send(o_far, [(1, 3)])
    near = shift(o_near, 1)
    mean, stat = call(
        own, (shape((rows, width), f32), shape((rows, LANES), f32)), 9, name="own"
    )(lengths, queries, keys, value, k1, va, vb, k2, v2)
    attended = call(merge, shape((rows, width), bf16), 4, 0, name="merge")(mean, stat, near, far)
    return value, attended


def solution(mesh):
    placed = (
        P(None, ("groups", "ctx"), "tp"),
        P(None, None, "tp"),
        P("tp", None),
        P("tp", None),
        P("tp"),
        P("groups"),
        P(("groups", "ctx"), "tp"),
        P(("groups", "ctx"), "tp"),
    )
    return jax.shard_map(
        shards,
        mesh=mesh,
        in_specs=placed,
        out_specs=(P(("groups", "ctx"), "tp"), P(("groups", "ctx"), "tp")),
        check_vma=False,
    )
```

```python
import functools
import math

import jax
import jax.numpy as jnp
from jax import lax
from jax.experimental import pallas as pl
from jax.experimental.pallas import tpu as pltpu
from jax.sharding import PartitionSpec as P


HEAD_DIM = 128
SHORT = 3
LANES = 128
NEG = -1e30


SMEM = pl.BlockSpec(memory_space=pltpu.SMEM)
VMEM = pl.BlockSpec(memory_space=pltpu.VMEM)
HBM = pl.BlockSpec(memory_space=pltpu.HBM)
SLOT = 32


def ends_of(lengths_ref):
    ends, total = [], jnp.int32(0)
    for r in range(lengths_ref.shape[0]):
        total = total + lengths_ref[r]
        ends.append(total)
    return ends


def start_of(place, ends):
    start = jnp.zeros_like(place)
    for end in ends:
        start = jnp.where(place >= end, end, start)
    return start


def end_of(place, ends):
    stop = ends[-1]
    for end in reversed(ends):
        stop = jnp.where(place < end, end, stop)
    return stop


def call(body, out, n_in, n_smem=1, scratch=(), flops=10**7, moved=4 * 10**6, space=VMEM):
    return pl.pallas_call(
        body,
        out_shape=out,
        in_specs=[SMEM] * n_smem + [space] * (n_in - n_smem),
        out_specs=jax.tree.map(lambda _: VMEM, out),
        scratch_shapes=list(scratch),
        compiler_params=pltpu.CompilerParams(vmem_limit_bytes=16 << 20),
        cost_estimate=pl.CostEstimate(flops=flops, bytes_accessed=moved, transcendentals=0),
    )


def hyena_local(lengths_ref, streams_ref, rim_ref, taps_ref, decay_ref, residue_ref, skip_ref,
                gate_ref, long_ref, state_ref, step_ref, block_ref, low_ref, high_ref,
                mixed_ref, gain_ref, final_ref):
    rows, width = gate_ref.shape
    modes = decay_ref.shape[0]
    tiles = width // LANES
    half = width // 2
    index = lax.axis_index("ctx")
    first = index * rows
    ends = ends_of(lengths_ref)

    row = lax.broadcasted_iota(jnp.int32, (rows, LANES), 0)
    place = row + first
    start = start_of(place, ends)
    inside = [None] + [(place - i >= start).astype(jnp.float32) for i in range(1, SHORT)]

    for j in range(tiles):
        lanes = slice(j * LANES, (j + 1) * LANES)
        filtered = []
        for s in range(3):
            x = streams_ref[s, :, lanes].astype(jnp.float32)
            rim = rim_ref[s, :, lanes].astype(jnp.float32)
            total = taps_ref[0, s : s + 1, lanes] * x
            for i in range(1, SHORT):
                moved = pltpu.roll(x, i, 0)
                for k in range(i):
                    moved = jnp.where(row == k, rim[SHORT - 1 - i + k : SHORT - i + k, :], moved)
                total = total + taps_ref[i, s : s + 1, lanes] * moved * inside[i]
            filtered.append(total)
        gate_ref[:, lanes] = filtered[0]
        mixed_ref[pl.ds(j, rows, stride=tiles), :] = filtered[1] * filtered[2]
        rate = decay_ref[:, lanes]
        step_ref[pl.ds(j, modes, stride=tiles), :] = jnp.exp(-rate)
        block_ref[pl.ds(j, modes, stride=tiles), :] = jnp.exp(-rate * rows)
        gain_ref[pl.ds(j, modes, stride=tiles), :] = residue_ref[:, lanes]

    for h in range(tiles // 8):
        decay = [step_ref[m * tiles + h * 8 : m * tiles + h * 8 + 8, :] for m in range(modes)]
        gain = [gain_ref[m * tiles + h * 8 : m * tiles + h * 8 + 8, :] for m in range(modes)]
        skip = skip_ref[h * 8 : h * 8 + 8, :]

        def advance(t, state):
            at = pl.ds(pl.multiple_of(t * tiles + h * 8, 8), 8)
            x = mixed_ref[at, :]
            state = tuple(s * d + g * x for s, d, g in zip(state, decay, gain))
            terms = list(state) + [skip * x]
            while len(terms) > 1:
                terms = [a + b for a, b in zip(terms[::2], terms[1::2])] + (
                    [terms[-1]] if len(terms) % 2 else []
                )
            long_ref[at, :] = terms[0]
            return state

        low = jnp.int32(0)
        for end in ends:
            high = jnp.clip(end - first, 0, rows)
            low_row = low

            def four(g, state, low_row=low_row):
                for u in range(4):
                    state = advance(low_row + g * 4 + u, state)
                return state

            groups = lax.shift_right_logical(high - low_row, 2)
            state = tuple(jnp.zeros((8, LANES), jnp.float32) for _ in range(modes))
            state = lax.fori_loop(0, groups, four, state)
            state = lax.fori_loop(low_row + groups * 4, high, advance, state)

            @pl.when((low_row < high) & (high == rows))
            def _(state=state):
                for m in range(modes):
                    final_ref[m * tiles + h * 8 : m * tiles + h * 8 + 8, :] = state[m]

            low = high
    state_ref[...] = final_ref[...].astype(state_ref.dtype)

    @pl.when(index == 0)
    def _():
        for j in range(tiles):
            lanes = slice(j * LANES, (j + 1) * LANES)
            value = gate_ref[:, lanes] * long_ref[pl.ds(j, rows, stride=tiles), :]
            out, at = (low_ref, j) if j * LANES < half else (high_ref, j - tiles // 2)
            out[:, at * LANES : (at + 1) * LANES] = value.astype(out.dtype)


def hyena_cross(hops, lengths_ref, step_ref, block_ref, long_ref, gate_ref, *refs):
    parts = refs[: len(hops)]
    value_ref, *halves, cross_ref = refs[len(hops) :]
    rows, width = gate_ref.shape
    tiles = width // LANES
    modes = step_ref.shape[0] // tiles
    index = lax.axis_index("ctx")
    first = index * rows
    ends = ends_of(lengths_ref)
    start = start_of(first - 1, ends)
    count = jnp.where(index > 0, jnp.clip(end_of(first - 1, ends) - first, 0, rows), 0)
    keeps = [
        ((first - 1 - hop * rows >= start) & (index > hop)).astype(jnp.float32) for hop in hops
    ]

    @pl.when(count > 0)
    def _():
        for h in range(tiles // 8):
            decay, incoming = [], []
            for m in range(modes):
                at = slice(m * tiles + h * 8, m * tiles + h * 8 + 8)
                decay.append(step_ref[at, :])
                total, factor = None, None
                for hop, keep, part in zip(hops, keeps, parts):
                    term = part[at, :].astype(jnp.float32) * keep
                    if hop:
                        factor = block_ref[at, :] if factor is None else factor * block_ref[at, :]
                        term = term * factor
                    total = term if total is None else total + term
                incoming.append(total)

            def advance(t, state):
                at = pl.ds(pl.multiple_of(t * tiles + h * 8, 8), 8)
                state = tuple(s * d for s, d in zip(state, decay))
                terms = list(state)
                while len(terms) > 1:
                    terms = [a + b for a, b in zip(terms[::2], terms[1::2])] + (
                        [terms[-1]] if len(terms) % 2 else []
                    )
                cross_ref[at, :] = terms[0]
                return state

            def four(g, state):
                for u in range(4):
                    state = advance(g * 4 + u, state)
                return state

            groups = lax.shift_right_logical(count, 2)
            state = lax.fori_loop(0, groups, four, tuple(incoming))
            lax.fori_loop(groups * 4, count, advance, state)

    row = lax.broadcasted_iota(jnp.int32, (rows, LANES), 0)
    reached = row < count
    for j in range(tiles):
        lanes = slice(j * LANES, (j + 1) * LANES)
        every = pl.ds(j, rows, stride=tiles)
        long = long_ref[every, :] + jnp.where(reached, cross_ref[every, :], 0.0)
        value_ref[:, lanes] = (gate_ref[:, lanes] * long).astype(value_ref.dtype)

    if halves:
        near_ref, other_ref = halves
        odd = index % 2 == 1
        copy_half(value_ref, near_ref, odd)
        copy_half(value_ref, other_ref, jnp.logical_not(odd))


def copy_half(source_ref, target_ref, lower):
    half = target_ref.shape[1]

    @pl.when(lower)
    def _():
        target_ref[...] = source_ref[:, :half]

    @pl.when(jnp.logical_not(lower))
    def _():
        target_ref[...] = source_ref[:, half:]


def pack(streams_ref, queries_ref, keys_ref, rim_ref, q_near, q_far, k_near, k_far, tail_ref, sems):
    reach_back = SHORT - 1
    rows, half = q_far.shape
    tail = tail_ref.shape[1]
    even = 1 - lax.axis_index("ctx") % 2
    near = pl.ds(pl.multiple_of(even * half, half), half)
    copies = [
        pltpu.make_async_copy(source, target, sems.at[i])
        for i, (source, target) in enumerate((
            (streams_ref.at[:, rows - tail :, :], tail_ref),
            (keys_ref.at[:, near], k_near),
            (keys_ref.at[:, :half], k_far),
            (queries_ref.at[:, near], q_near),
            (queries_ref.at[:, half:], q_far),
        ))
    ]
    for copy in copies:
        copy.start()
    copies[0].wait()
    rim_ref[...] = tail_ref[:, tail - reach_back :, :]
    for copy in copies[1:]:
        copy.wait()


def biases(query_block, key_blocks, rows, ends):
    place = query_block * rows + lax.broadcasted_iota(jnp.int32, (rows, rows), 0)
    start = start_of(place, ends)
    out = []
    for block in key_blocks:
        key = block * rows + lax.broadcasted_iota(jnp.int32, (rows, rows), 1)
        out.append(jnp.where((key >= start) & (key <= place), 0.0, NEG))
    return out


def one_head(query, pairs, bias):
    scale = 1.0 / math.sqrt(HEAD_DIM)
    base2 = scale * math.log2(math.e)
    dims = (((1,), (1,)), ((), ()))
    scores = [
        lax.dot_general(query, key, dims, preferred_element_type=jnp.float32) + b
        for (key, _), b in zip(pairs, bias)
    ]
    top = scores[0]
    for s in scores[1:]:
        top = jnp.maximum(top, s)
    top = jnp.max(top, axis=1, keepdims=True)
    weights = [jnp.exp2((s - top) * base2) for s in scores]
    total = weights[0]
    for w in weights[1:]:
        total = total + w
    total = jnp.sum(total, axis=1, keepdims=True)
    summed = None
    for w, (_, value) in zip(weights, pairs):
        part = jnp.dot(w.astype(jnp.bfloat16), value, preferred_element_type=jnp.float32)
        summed = part if summed is None else summed + part
    return summed / total, top * scale + jnp.log(total)


def cut(ref, h):
    return ref[:, h * HEAD_DIM : (h + 1) * HEAD_DIM]


def split3(x):
    a = x.astype(jnp.bfloat16)
    rest = x - a.astype(jnp.float32)
    b = rest.astype(jnp.bfloat16)
    c = (rest - b.astype(jnp.float32)).astype(jnp.bfloat16)
    return a, b, c


def attend(query_block, query_ref, query_at, sources, rows, count, ends, write):
    bias = biases(query_block, [block for block, _, _, _ in sources], rows, ends)
    for h in range(count):
        pairs = [(cut(keys, at + h), cut(values, h)) for _, keys, at, values in sources]
        write(h, *one_head(cut(query_ref, query_at + h), pairs, bias))


def serve(query_block, query_ref, sources, ends, out_ref):
    rows, half = query_ref.shape
    lane = lax.broadcasted_iota(jnp.int32, (rows, LANES), 1)
    stats = [jnp.zeros((rows, LANES), jnp.float32)]

    def write(h, mean, log_total):
        out_ref[:, h * HEAD_DIM : (h + 1) * HEAD_DIM] = mean.astype(out_ref.dtype)
        for k, piece in enumerate(split3(log_total)):
            stats[0] = jnp.where(lane == SLOT * k + h, piece.astype(jnp.float32), stats[0])

    attend(query_block, query_ref, 0, sources, rows, half // HEAD_DIM, ends, write)
    out_ref[:, half:] = stats[0].astype(out_ref.dtype)


def hub_far(lengths_ref, q2_ref, key_ref, other_ref, k1_ref, va_ref, far_ref):
    count = q2_ref.shape[1] // HEAD_DIM

    @pl.when(lax.axis_index("ctx") == 1)
    def _():
        sources = [(1, key_ref, count, other_ref), (0, k1_ref, 0, va_ref)]
        serve(3, q2_ref, sources, ends_of(lengths_ref), far_ref)


def hub_near(lengths_ref, q1_ref, key_ref, other_ref, k1_ref, va_ref, vb_ref, k2_ref, v2_ref,
             near_ref):
    count = q1_ref.shape[1] // HEAD_DIM
    index = lax.axis_index("ctx")
    ends = ends_of(lengths_ref)

    @pl.when(index == 0)
    def _():
        serve(1, q1_ref, [(0, key_ref, 0, other_ref)], ends, near_ref)

    @pl.when(index == 1)
    def _():
        sources = [(1, key_ref, count, other_ref), (0, k1_ref, 0, va_ref)]
        serve(2, q1_ref, sources, ends, near_ref)

    @pl.when(index == 2)
    def _():
        sources = [(2, key_ref, 0, other_ref), (1, k1_ref, 0, vb_ref), (0, k2_ref, 0, v2_ref)]
        serve(3, q1_ref, sources, ends, near_ref)


def own_half(query_ref, key_ref, mean_ref, stat_ref, ends, base, values, more=()):
    rows, width = query_ref.shape
    index = lax.axis_index("ctx")
    lane = lax.broadcasted_iota(jnp.int32, (rows, LANES), 1)
    stats = [jnp.zeros((rows, LANES), jnp.float32)]

    def write(h, mean, log_total):
        mean_ref[:, (base + h) * HEAD_DIM : (base + h + 1) * HEAD_DIM] = mean
        stats[0] = jnp.where(lane == h, log_total, stats[0])

    sources = [(index, key_ref, base, values), *more]
    attend(index, query_ref, base, sources, rows, width // HEAD_DIM // 2, ends, write)
    stat_ref[:, (LANES if base else 0) : (2 * LANES if base else LANES)] = stats[0]


def own_early(lengths_ref, query_ref, key_ref, near_ref, other_ref, mean_ref, stat_ref):
    count = query_ref.shape[1] // HEAD_DIM // 2
    index = lax.axis_index("ctx")
    run = functools.partial(
        own_half, query_ref, key_ref, mean_ref, stat_ref, ends_of(lengths_ref)
    )

    @pl.when(index == 0)
    def _():
        run(0, other_ref)

    @pl.when(index == 3)
    def _():
        run(0, near_ref)

    @pl.when(index % 2 == 0)
    def _():
        run(count, near_ref)


def own_late(lengths_ref, query_ref, key_ref, near_ref, other_ref, k1_ref, va_ref, vb_ref, k2_ref,
             v2_ref, mean_ref, stat_ref):
    count = query_ref.shape[1] // HEAD_DIM // 2
    index = lax.axis_index("ctx")
    run = functools.partial(
        own_half, query_ref, key_ref, mean_ref, stat_ref, ends_of(lengths_ref)
    )

    @pl.when(index == 1)
    def _():
        run(0, near_ref)
        run(count, other_ref, [(0, k1_ref, 0, va_ref)])

    @pl.when(index == 2)
    def _():
        run(0, other_ref, [(1, k1_ref, 0, vb_ref), (0, k2_ref, 0, v2_ref)])

    @pl.when(index == 3)
    def _():
        run(count, other_ref, [(2, k1_ref, 0, vb_ref)])


def merge(early_ref, early_stat, late_ref, late_stat, near_ref, far_ref, out_ref):
    _, width = early_ref.shape
    half = width // 2
    count = half // HEAD_DIM
    index = lax.axis_index("ctx")

    def join(base, mean_ref, stat_ref, other_ref):
        here = stat_ref[:, (LANES if base else 0) : (2 * LANES if base else LANES)]
        there = other_ref[:, half:].astype(jnp.float32)
        there = there + pltpu.roll(there, LANES - SLOT, 1) + pltpu.roll(there, LANES - 2 * SLOT, 1)
        top = jnp.maximum(here, there)
        a, b = jnp.exp(here - top), jnp.exp(there - top)
        norm = 1.0 / (a + b)
        a, b = a * norm, b * norm
        for h in range(count):
            at = slice((h + base) * HEAD_DIM, (h + base + 1) * HEAD_DIM)
            other = cut(other_ref, h).astype(jnp.float32)
            out_ref[:, at] = (
                mean_ref[:, at] * a[:, h : h + 1] + other * b[:, h : h + 1]
            ).astype(out_ref.dtype)

    def keep(base, mean_ref):
        at = slice(base * HEAD_DIM, (base + count) * HEAD_DIM)
        out_ref[:, at] = mean_ref[:, at].astype(out_ref.dtype)

    @pl.when(index == 0)
    def _():
        keep(0, early_ref)
        keep(count, early_ref)

    @pl.when(index == 1)
    def _():
        join(0, late_ref, late_stat, near_ref)
        keep(count, late_ref)

    @pl.when(index == 2)
    def _():
        keep(0, late_ref)
        join(count, early_ref, early_stat, near_ref)

    @pl.when(index == 3)
    def _():
        join(0, early_ref, early_stat, near_ref)
        join(count, late_ref, late_stat, far_ref)


def doc_of(places, ends):
    return jnp.sum((places[:, None] >= ends[None, :]).astype(jnp.int32), axis=1)


def gathered_attention(lengths, queries, keys, values):
    rows, width = queries.shape
    heads_here = width // HEAD_DIM
    ends = jnp.cumsum(lengths)
    places = lax.axis_index("ctx") * rows + jnp.arange(rows, dtype=jnp.int32)
    piece = lax.all_gather(jnp.stack([keys, values]), "ctx", axis=1, tiled=True)
    count = piece.shape[1]
    key_places = jnp.arange(count, dtype=jnp.int32)
    allowed = (key_places[None, :] <= places[:, None]) & (
        doc_of(key_places, ends)[None, :] == doc_of(places, ends)[:, None]
    )
    scores = jnp.einsum(
        "qhd,khd->hqk",
        queries.reshape(rows, heads_here, HEAD_DIM),
        piece[0].reshape(count, heads_here, HEAD_DIM),
        preferred_element_type=jnp.float32,
    )
    masked = jnp.where(allowed[None], scores * (1.0 / math.sqrt(HEAD_DIM)), NEG)
    weight = jnp.exp(masked - jnp.max(masked, axis=2, keepdims=True))
    total = jnp.sum(weight, axis=2)
    summed = jnp.einsum(
        "hqk,khd->hqd",
        weight.astype(jnp.bfloat16),
        piece[1].reshape(count, heads_here, HEAD_DIM),
        preferred_element_type=jnp.float32,
    )
    return (summed / total[..., None]).transpose(1, 0, 2).reshape(rows, width).astype(jnp.bfloat16)


def send(value, pairs):
    return lax.ppermute(value, "ctx", pairs)


def shift(value, steps):
    count = lax.axis_size("ctx")
    return send(value, [(i, i + steps) for i in range(count) if 0 <= i + steps < count])


def in_pairs(ctx, width):
    count = width // HEAD_DIM
    return ctx == 4 and count % 2 == 0 and count // 2 <= SLOT


def shards(streams, short_filter, decay_rate, residue, skip_gain, lengths, queries, keys):
    f32, bf16 = jnp.float32, jnp.bfloat16
    shape = jax.ShapeDtypeStruct
    rows, width = streams.shape[1:]
    half = width // 2
    modes = decay_rate.shape[1]
    tiles = width // LANES
    ctx = lax.axis_size("ctx")
    paired = in_pairs(ctx, width)
    halves = shape((rows, half), bf16)

    if paired:
        rim, q_near, q_far, k_near, k_far = call(
            pack, (shape((3, SHORT - 1, width), bf16), halves, halves, halves, halves), 3, 0,
            scratch=[pltpu.VMEM((3, 16, width), bf16), pltpu.SemaphoreType.DMA((5,))],
            space=HBM,
        )(*(pltpu.with_memory_space_constraint(a, pltpu.HBM) for a in (streams, queries, keys)))
        rim = shift(rim, 1)
        q1 = shift(q_near, -1)
        q2 = send(q_far, [(3, 1)])
        k1 = shift(k_near, 1)
        k2 = send(k_far, [(0, 2)])
    else:
        rim = shift(streams[:, rows - SHORT + 1 :, :], 1)

    states = (modes * tiles, LANES)
    gate, long, state, step, block, low, high = call(
        hyena_local,
        (
            shape((rows, width), f32),
            shape((rows * tiles, LANES), f32),
            shape(states, bf16),
            shape(states, f32),
            shape(states, f32),
            halves,
            halves,
        ),
        7,
        scratch=[
            pltpu.VMEM((rows * tiles, LANES), f32),
            pltpu.VMEM(states, f32),
            pltpu.VMEM(states, f32),
        ],
    )(lengths, streams, rim, short_filter, decay_rate.T, residue.T, skip_gain.reshape(tiles, LANES))

    if paired:
        va = send(high, [(0, 1)])
        v2 = send(low, [(0, 2)])
        hops = tuple(range(ctx - 1))
        parts = [shift(state, hop + 1) for hop in hops]
    else:
        every = lax.all_gather(state, "ctx").astype(f32)
        ends = jnp.cumsum(lengths)
        before = lax.axis_index("ctx") * rows - 1
        lasts = (jnp.arange(ctx, dtype=jnp.int32) + 1) * rows - 1
        same = (lasts <= before) & (
            doc_of(lasts, ends) == doc_of(jnp.reshape(before, (1,)), ends)
        )
        factor = jnp.where(same, (before - lasts) // rows, 0).astype(f32)
        weight = same.astype(f32)[:, None, None] * block[None] ** factor[:, None, None]
        parts = [jnp.sum(weight * every, axis=0)]
        hops = (0,)

    value, *split = call(
        functools.partial(hyena_cross, hops),
        (shape((rows, width), bf16),) + ((halves, halves) if paired else ()),
        5 + len(hops),
        scratch=[pltpu.VMEM((rows * tiles, LANES), f32)],
    )(lengths, step, block, long, gate, *parts)

    if not paired:
        return value, gathered_attention(lengths, queries, keys, value)

    near, other = split
    vb = send(near, [(1, 2), (2, 3)])
    wide = shape((rows, half + LANES), bf16)
    o_far = call(hub_far, wide, 6)(lengths, q2, keys, other, k1, va)
    far = send(o_far, [(1, 3)])
    means = (shape((rows, width), f32), shape((rows, 2 * LANES), f32))
    early = call(own_early, means, 5)(lengths, queries, keys, near, other)
    o_near = call(hub_near, wide, 9)(
        lengths, q1, keys, other, k1, va, vb, k2, v2
    )
    last = shift(o_near, 1)
    late = call(own_late, means, 10)(lengths, queries, keys, near, other, k1, va, vb, k2, v2)
    attended = call(merge, shape((rows, width), bf16), 6, 0)(
        *early, *late, last, far
    )
    return value, attended


def solution(mesh):
    placed = (
        P(None, ("groups", "ctx"), "tp"),
        P(None, None, "tp"),
        P("tp", None),
        P("tp", None),
        P("tp"),
        P("groups"),
        P(("groups", "ctx"), "tp"),
        P(("groups", "ctx"), "tp"),
    )

    return jax.shard_map(
        shards,
        mesh=mesh,
        in_specs=placed,
        out_specs=(P(("groups", "ctx"), "tp"), P(("groups", "ctx"), "tp")),
        check_vma=False,
    )
```

```python
import functools
import math

import jax
import jax.numpy as jnp
from jax import lax
from jax.experimental import pallas as pl
from jax.experimental.pallas import tpu as pltpu
from jax.sharding import PartitionSpec as P


HEAD_DIM = 128
SHORT = 3
LANES = 128
NEG = -1e30


SMEM = pl.BlockSpec(memory_space=pltpu.SMEM)
VMEM = pl.BlockSpec(memory_space=pltpu.VMEM)
HBM = pl.BlockSpec(memory_space=pltpu.HBM)
SLOT = 32


def ends_of(lengths_ref):
    ends, total = [], jnp.int32(0)
    for r in range(lengths_ref.shape[0]):
        total = total + lengths_ref[r]
        ends.append(total)
    return ends


def start_of(place, ends):
    start = jnp.zeros_like(place)
    for end in ends:
        start = jnp.where(place >= end, end, start)
    return start


def end_of(place, ends):
    stop = ends[-1]
    for end in reversed(ends):
        stop = jnp.where(place < end, end, stop)
    return stop


def call(body, out, n_in, n_smem=1, scratch=(), flops=10**7, moved=4 * 10**6, space=VMEM):
    return pl.pallas_call(
        body,
        out_shape=out,
        in_specs=[SMEM] * n_smem + [space] * (n_in - n_smem),
        out_specs=jax.tree.map(lambda _: VMEM, out),
        scratch_shapes=list(scratch),
        compiler_params=pltpu.CompilerParams(vmem_limit_bytes=16 << 20),
        cost_estimate=pl.CostEstimate(flops=flops, bytes_accessed=moved, transcendentals=0),
    )


def hyena_local(lengths_ref, streams_ref, rim_ref, taps_ref, decay_ref, residue_ref, skip_ref,
                gate_ref, long_ref, state_ref, step_ref, block_ref,
                mixed_ref, gain_ref, final_ref):
    rows, width = gate_ref.shape
    modes = decay_ref.shape[0]
    tiles = width // LANES
    index = lax.axis_index("ctx")
    first = index * rows
    ends = ends_of(lengths_ref)

    row = lax.broadcasted_iota(jnp.int32, (rows, LANES), 0)
    place = row + first
    start = start_of(place, ends)
    inside = [None] + [(place - i >= start).astype(jnp.float32) for i in range(1, SHORT)]

    for j in range(tiles):
        lanes = slice(j * LANES, (j + 1) * LANES)
        filtered = []
        for s in range(3):
            x = streams_ref[s, :, lanes].astype(jnp.float32)
            rim = rim_ref[s, :, lanes].astype(jnp.float32)
            total = taps_ref[0, s : s + 1, lanes] * x
            for i in range(1, SHORT):
                moved = pltpu.roll(x, i, 0)
                for k in range(i):
                    moved = jnp.where(row == k, rim[SHORT - 1 - i + k : SHORT - i + k, :], moved)
                total = total + taps_ref[i, s : s + 1, lanes] * moved * inside[i]
            filtered.append(total)
        gate_ref[:, lanes] = filtered[0]
        mixed_ref[pl.ds(j, rows, stride=tiles), :] = filtered[1] * filtered[2]
        rate = decay_ref[:, lanes]
        step_ref[pl.ds(j, modes, stride=tiles), :] = jnp.exp(-rate)
        block_ref[pl.ds(j, modes, stride=tiles), :] = jnp.exp(-rate * rows)
        gain_ref[pl.ds(j, modes, stride=tiles), :] = residue_ref[:, lanes]

    for h in range(tiles // 8):
        decay = [step_ref[m * tiles + h * 8 : m * tiles + h * 8 + 8, :] for m in range(modes)]
        gain = [gain_ref[m * tiles + h * 8 : m * tiles + h * 8 + 8, :] for m in range(modes)]
        skip = skip_ref[h * 8 : h * 8 + 8, :]

        def advance(t, state):
            at = pl.ds(pl.multiple_of(t * tiles + h * 8, 8), 8)
            x = mixed_ref[at, :]
            state = tuple(s * d + g * x for s, d, g in zip(state, decay, gain))
            terms = list(state) + [skip * x]
            while len(terms) > 1:
                terms = [a + b for a, b in zip(terms[::2], terms[1::2])] + (
                    [terms[-1]] if len(terms) % 2 else []
                )
            long_ref[at, :] = terms[0]
            return state

        low = jnp.int32(0)
        for end in ends:
            high = jnp.clip(end - first, 0, rows)
            low_row = low

            def four(g, state, low_row=low_row):
                for u in range(4):
                    state = advance(low_row + g * 4 + u, state)
                return state

            groups = lax.shift_right_logical(high - low_row, 2)
            state = tuple(jnp.zeros((8, LANES), jnp.float32) for _ in range(modes))
            state = lax.fori_loop(0, groups, four, state)
            state = lax.fori_loop(low_row + groups * 4, high, advance, state)

            @pl.when((low_row < high) & (high == rows))
            def _(state=state):
                for m in range(modes):
                    final_ref[m * tiles + h * 8 : m * tiles + h * 8 + 8, :] = state[m]

            low = high
    state_ref[...] = final_ref[...].astype(state_ref.dtype)


def hyena_cross(hops, lengths_ref, step_ref, block_ref, long_ref, gate_ref, *refs):
    parts = refs[: len(hops)]
    value_ref, cross_ref = refs[len(hops) :]
    rows, width = gate_ref.shape
    tiles = width // LANES
    modes = step_ref.shape[0] // tiles
    index = lax.axis_index("ctx")
    first = index * rows
    ends = ends_of(lengths_ref)
    start = start_of(first - 1, ends)
    count = jnp.where(index > 0, jnp.clip(end_of(first - 1, ends) - first, 0, rows), 0)
    keeps = [
        ((first - 1 - hop * rows >= start) & (index > hop)).astype(jnp.float32) for hop in hops
    ]

    @pl.when(count > 0)
    def _():
        for h in range(tiles // 8):
            decay, incoming = [], []
            for m in range(modes):
                at = slice(m * tiles + h * 8, m * tiles + h * 8 + 8)
                decay.append(step_ref[at, :])
                total, factor = None, None
                for hop, keep, part in zip(hops, keeps, parts):
                    term = part[at, :].astype(jnp.float32) * keep
                    if hop:
                        factor = block_ref[at, :] if factor is None else factor * block_ref[at, :]
                        term = term * factor
                    total = term if total is None else total + term
                incoming.append(total)

            def advance(t, state):
                at = pl.ds(pl.multiple_of(t * tiles + h * 8, 8), 8)
                state = tuple(s * d for s, d in zip(state, decay))
                terms = list(state)
                while len(terms) > 1:
                    terms = [a + b for a, b in zip(terms[::2], terms[1::2])] + (
                        [terms[-1]] if len(terms) % 2 else []
                    )
                cross_ref[at, :] = terms[0]
                return state

            def four(g, state):
                for u in range(4):
                    state = advance(g * 4 + u, state)
                return state

            groups = lax.shift_right_logical(count, 2)
            state = lax.fori_loop(0, groups, four, tuple(incoming))
            lax.fori_loop(groups * 4, count, advance, state)

    row = lax.broadcasted_iota(jnp.int32, (rows, LANES), 0)
    reached = row < count
    for j in range(tiles):
        lanes = slice(j * LANES, (j + 1) * LANES)
        every = pl.ds(j, rows, stride=tiles)
        long = long_ref[every, :] + jnp.where(reached, cross_ref[every, :], 0.0)
        value_ref[:, lanes] = (gate_ref[:, lanes] * long).astype(value_ref.dtype)


def tree_sum(terms):
    while len(terms) > 1:
        odd = [terms[-1]] if len(terms) % 2 else []
        terms = [a + b for a, b in zip(terms[::2], terms[1::2])] + odd
    return terms[0]


def stage(me, last, lengths_ref, streams_ref, taps_ref, decay_ref, residue_ref, skip_ref, *refs):
    refs = list(refs)
    carry_ref = refs.pop(0) if me else None
    near_ref, other_ref = refs[:2]
    next_ref = None if last else refs[2]
    gate_ref, mixed_ref, long_ref, step_ref, gain_ref, carried_ref, shifted_ref = refs[-7:]
    rows, half = near_ref.shape
    width = 2 * half
    modes = decay_ref.shape[0]
    tiles = width // LANES
    states = modes * tiles
    first = me * rows
    reach_back = SHORT - 1

    def run():
        ends = ends_of(lengths_ref)
        start = start_of(jnp.int32(first), ends)
        goes_on = [(start <= first - i).astype(jnp.float32) for i in range(1, SHORT)]
        if me:
            carried_ref[...] = carry_ref[...].astype(jnp.float32)
        edges = {}
        if me:
            for s in range(3):
                for k in range(1, SHORT):
                    at = states + (s * reach_back + reach_back - k) * tiles
                    edges[s, k] = carried_ref[at : at + tiles, :] * goes_on[k - 1]
        for j in range(tiles):
            lanes = slice(j * LANES, (j + 1) * LANES)
            filtered = []
            for s in range(3):
                x = streams_ref[s, :, lanes].astype(jnp.float32)
                total = taps_ref[0, s : s + 1, lanes] * x
                for i in range(1, SHORT):
                    buffer = shifted_ref.at[j % 2, s, i - 1]
                    buffer[8 : 8 + rows, :] = x
                    for k in range(1, i + 1):
                        edge = edges[s, k][j : j + 1, :] if me else jnp.zeros((1, LANES), jnp.float32)
                        buffer[8 - k : 9 - k, :] = edge
                    for end in ends[:-1]:
                        inside = (end > first) & (end < first + rows)
                        for k in range(1, i + 1):
                            at = jnp.where(inside, 8 + end - first - k, rows + 8)
                            buffer[pl.ds(at, 1), :] = jnp.zeros((1, LANES), jnp.float32)
                    total = total + taps_ref[i, s : s + 1, lanes] * buffer[8 - i : 8 - i + rows, :]
                filtered.append(total)
                if not last:
                    for k in range(reach_back):
                        at = states + (s * reach_back + k) * tiles + j
                        row = rows - reach_back + k
                        carried_ref[at : at + 1, :] = x[row : row + 1, :]
            gate_ref[:, lanes] = filtered[0]
            mixed_ref[pl.ds(j, rows, stride=tiles), :] = filtered[1] * filtered[2]
            step_ref[pl.ds(j, modes, stride=tiles), :] = jnp.exp(-decay_ref[:, lanes])
            gain_ref[pl.ds(j, modes, stride=tiles), :] = residue_ref[:, lanes]

        for h in range(tiles // 8):
            spots = [slice(m * tiles + h * 8, m * tiles + h * 8 + 8) for m in range(modes)]
            decay = [step_ref[at, :] for at in spots]
            gain = [gain_ref[at, :] for at in spots]
            skip = skip_ref[h * 8 : h * 8 + 8, :]

            def advance(t, state):
                at = pl.ds(pl.multiple_of(t * tiles + h * 8, 8), 8)
                x = mixed_ref[at, :]
                state = tuple(s * d + g * x for s, d, g in zip(state, decay, gain))
                long_ref[at, :] = tree_sum(list(state) + [skip * x])
                return state

            incoming = [carried_ref[at, :] * goes_on[0] for at in spots] if me else None
            low = jnp.int32(0)
            for end in ends:
                high = jnp.clip(end - first, 0, rows)

                def four(g, state, low=low):
                    for u in range(4):
                        state = advance(low + g * 4 + u, state)
                    return state

                groups = lax.shift_right_logical(high - low, 2)
                if me:
                    at_start = (low == 0).astype(jnp.float32)
                    state = tuple(s * at_start for s in incoming)
                else:
                    state = tuple(jnp.zeros((8, LANES), jnp.float32) for _ in spots)
                state = lax.fori_loop(0, groups, four, state)
                state = lax.fori_loop(low + groups * 4, high, advance, state)
                if not last:

                    @pl.when((low < high) & (high == rows))
                    def _(state=state):
                        for at, s in zip(spots, state):
                            carried_ref[at, :] = s

                low = high
        if not last:
            next_ref[...] = carried_ref[...].astype(next_ref.dtype)
        lower, upper = (near_ref, other_ref) if me % 2 else (other_ref, near_ref)
        for j in range(tiles):
            long = long_ref[pl.ds(j, rows, stride=tiles), :]
            value = gate_ref[:, j * LANES : (j + 1) * LANES] * long
            out, at = (lower, j) if j < tiles // 2 else (upper, j - tiles // 2)
            out[:, at * LANES : (at + 1) * LANES] = value.astype(out.dtype)

    pl.when(lax.axis_index("ctx") == me)(run)


def pack(queries_ref, keys_ref, *refs):
    count = (len(refs) - 5) // 2
    given, (q_near, q_far, k_near, k_far), held = refs[:count], refs[count:][:4], refs[count + 4 : -1]
    sems = refs[-1]
    half = q_far.shape[1]
    even = 1 - lax.axis_index("ctx") % 2
    near = pl.ds(pl.multiple_of(even * half, half), half)
    copies = [
        pltpu.make_async_copy(source, target, sems.at[i])
        for i, (source, target) in enumerate((
            *zip(given, held),
            (queries_ref.at[:, half:], q_far),
            (keys_ref.at[:, near], k_near),
            (keys_ref.at[:, :half], k_far),
            (queries_ref.at[:, near], q_near),
        ))
    ]
    for copy in copies:
        copy.start()
    for copy in copies:
        copy.wait()


def biases(query_block, key_blocks, rows, ends):
    place = query_block * rows + lax.broadcasted_iota(jnp.int32, (rows, rows), 0)
    start = start_of(place, ends)
    out = []
    for block in key_blocks:
        key = block * rows + lax.broadcasted_iota(jnp.int32, (rows, rows), 1)
        out.append(jnp.where((key >= start) & (key <= place), 0.0, NEG))
    return out


def one_head(query, keys, values, bias):
    scale = 1.0 / math.sqrt(HEAD_DIM)
    base2 = scale * math.log2(math.e)
    key = keys[0] if len(keys) == 1 else jnp.concatenate(keys, axis=0)
    value = values[0] if len(values) == 1 else jnp.concatenate(values, axis=0)
    scores = lax.dot_general(
        query, key, (((1,), (1,)), ((), ())), preferred_element_type=jnp.float32
    ) + bias
    top = jnp.max(scores, axis=1, keepdims=True)
    weights = jnp.exp2((scores - top) * base2)
    total = jnp.sum(weights, axis=1, keepdims=True)
    summed = jnp.dot(weights.astype(jnp.bfloat16), value, preferred_element_type=jnp.float32)
    return summed / total, top * scale + jnp.log(total)


def cut(ref, h):
    return ref[:, h * HEAD_DIM : (h + 1) * HEAD_DIM]


def split3(x):
    a = x.astype(jnp.bfloat16)
    rest = x - a.astype(jnp.float32)
    b = rest.astype(jnp.bfloat16)
    c = (rest - b.astype(jnp.float32)).astype(jnp.bfloat16)
    return a, b, c


def attend(query_block, query_ref, query_at, sources, rows, count, ends, write):
    bias = jnp.concatenate(
        biases(query_block, [block for block, _, _, _ in sources], rows, ends), axis=1
    )
    for h in range(count):
        held_keys = [cut(keys, at + h) for _, keys, at, _ in sources]
        held_values = [cut(values, h) for _, _, _, values in sources]
        write(h, *one_head(cut(query_ref, query_at + h), held_keys, held_values, bias))


def serve(query_block, query_ref, sources, ends, out_ref):
    rows, half = query_ref.shape
    lane = lax.broadcasted_iota(jnp.int32, (rows, LANES), 1)
    stats = [jnp.zeros((rows, LANES), jnp.float32)]

    def write(h, mean, log_total):
        out_ref[:, h * HEAD_DIM : (h + 1) * HEAD_DIM] = mean.astype(out_ref.dtype)
        for k, piece in enumerate(split3(log_total)):
            stats[0] = jnp.where(lane == SLOT * k + h, piece.astype(jnp.float32), stats[0])

    attend(query_block, query_ref, 0, sources, rows, half // HEAD_DIM, ends, write)
    out_ref[:, half:] = stats[0].astype(out_ref.dtype)


def hub_far(lengths_ref, q2_ref, key_ref, other_ref, k1_ref, va_ref, far_ref):
    count = q2_ref.shape[1] // HEAD_DIM

    @pl.when(lax.axis_index("ctx") == 1)
    def _():
        sources = [(1, key_ref, count, other_ref), (0, k1_ref, 0, va_ref)]
        serve(3, q2_ref, sources, ends_of(lengths_ref), far_ref)


def hub_mid(lengths_ref, q1_ref, key_ref, other0, other1, k1_ref, va_ref, near_ref):
    count = q1_ref.shape[1] // HEAD_DIM
    index = lax.axis_index("ctx")
    ends = ends_of(lengths_ref)

    @pl.when(index == 0)
    def _():
        serve(1, q1_ref, [(0, key_ref, 0, other0)], ends, near_ref)

    @pl.when(index == 1)
    def _():
        sources = [(1, key_ref, count, other1), (0, k1_ref, 0, va_ref)]
        serve(2, q1_ref, sources, ends, near_ref)


def hub_last(lengths_ref, q1_ref, key_ref, other_ref, k1_ref, vb_ref, k2_ref, v2_ref, near_ref):
    @pl.when(lax.axis_index("ctx") == 2)
    def _():
        sources = [(2, key_ref, 0, other_ref), (1, k1_ref, 0, vb_ref), (0, k2_ref, 0, v2_ref)]
        serve(3, q1_ref, sources, ends_of(lengths_ref), near_ref)


def own_half(query_ref, key_ref, mean_ref, stat_ref, ends, base, values, more=()):
    rows, width = query_ref.shape
    index = lax.axis_index("ctx")
    lane = lax.broadcasted_iota(jnp.int32, (rows, LANES), 1)
    stats = [jnp.zeros((rows, LANES), jnp.float32)]

    def write(h, mean, log_total):
        mean_ref[:, (base + h) * HEAD_DIM : (base + h + 1) * HEAD_DIM] = mean
        stats[0] = jnp.where(lane == h, log_total, stats[0])

    sources = [(index, key_ref, base, values), *more]
    attend(index, query_ref, base, sources, rows, width // HEAD_DIM // 2, ends, write)
    stat_ref[:, (LANES if base else 0) : (2 * LANES if base else LANES)] = stats[0]


def own_early(lengths_ref, query_ref, key_ref, k1_ref, va_ref, near0, near1, near2, other0, other1,
              mean_ref, stat_ref):
    count = query_ref.shape[1] // HEAD_DIM // 2
    index = lax.axis_index("ctx")
    run = functools.partial(
        own_half, query_ref, key_ref, mean_ref, stat_ref, ends_of(lengths_ref)
    )

    @pl.when(index == 0)
    def _():
        run(0, other0)
        run(count, near0)

    @pl.when(index == 1)
    def _():
        run(0, near1)
        run(count, other1, [(0, k1_ref, 0, va_ref)])

    @pl.when(index == 2)
    def _():
        run(count, near2)


def own_late(lengths_ref, query_ref, key_ref, k1_ref, vb_ref, vc_ref, k2_ref, v2_ref,
             near0, near1, near2, near3, other0, other1, other2, other3,
             value_ref, mean_ref, stat_ref):
    count = query_ref.shape[1] // HEAD_DIM // 2
    half = near0.shape[1]
    index = lax.axis_index("ctx")
    run = functools.partial(
        own_half, query_ref, key_ref, mean_ref, stat_ref, ends_of(lengths_ref)
    )
    for me, (lower, upper) in enumerate(
        ((other0, near0), (near1, other1), (other2, near2), (near3, other3))
    ):
        @pl.when(index == me)
        def _(lower=lower, upper=upper):
            value_ref[:, :half] = lower[...]
            value_ref[:, half:] = upper[...]

    @pl.when(index == 2)
    def _():
        run(0, other2, [(1, k1_ref, 0, vb_ref), (0, k2_ref, 0, v2_ref)])

    @pl.when(index == 3)
    def _():
        run(0, near3)
        run(count, other3, [(2, k1_ref, 0, vc_ref)])


def merge(early_ref, early_stat, late_ref, late_stat, near_a, near_b, far_ref, out_ref):
    _, width = early_ref.shape
    half = width // 2
    count = half // HEAD_DIM
    index = lax.axis_index("ctx")

    def join(base, mean_ref, stat_ref, other_ref):
        here = stat_ref[:, (LANES if base else 0) : (2 * LANES if base else LANES)]
        there = other_ref[:, half:].astype(jnp.float32)
        there = there + pltpu.roll(there, LANES - SLOT, 1) + pltpu.roll(there, LANES - 2 * SLOT, 1)
        top = jnp.maximum(here, there)
        a, b = jnp.exp(here - top), jnp.exp(there - top)
        norm = 1.0 / (a + b)
        a, b = a * norm, b * norm
        for h in range(count):
            at = slice((h + base) * HEAD_DIM, (h + base + 1) * HEAD_DIM)
            other = cut(other_ref, h).astype(jnp.float32)
            out_ref[:, at] = (
                mean_ref[:, at] * a[:, h : h + 1] + other * b[:, h : h + 1]
            ).astype(out_ref.dtype)

    def keep(base, mean_ref):
        at = slice(base * HEAD_DIM, (base + count) * HEAD_DIM)
        out_ref[:, at] = mean_ref[:, at].astype(out_ref.dtype)

    @pl.when(index == 0)
    def _():
        keep(0, early_ref)
        keep(count, early_ref)

    @pl.when(index == 1)
    def _():
        join(0, early_ref, early_stat, near_a)
        keep(count, early_ref)

    @pl.when(index == 2)
    def _():
        keep(0, late_ref)
        join(count, early_ref, early_stat, near_a)

    @pl.when(index == 3)
    def _():
        join(0, late_ref, late_stat, near_b)
        join(count, late_ref, late_stat, far_ref)


def doc_of(places, ends):
    return jnp.sum((places[:, None] >= ends[None, :]).astype(jnp.int32), axis=1)


def gathered_attention(lengths, queries, keys, values):
    rows, width = queries.shape
    heads_here = width // HEAD_DIM
    ends = jnp.cumsum(lengths)
    places = lax.axis_index("ctx") * rows + jnp.arange(rows, dtype=jnp.int32)
    piece = lax.all_gather(jnp.stack([keys, values]), "ctx", axis=1, tiled=True)
    count = piece.shape[1]
    key_places = jnp.arange(count, dtype=jnp.int32)
    allowed = (key_places[None, :] <= places[:, None]) & (
        doc_of(key_places, ends)[None, :] == doc_of(places, ends)[:, None]
    )
    scores = jnp.einsum(
        "qhd,khd->hqk",
        queries.reshape(rows, heads_here, HEAD_DIM),
        piece[0].reshape(count, heads_here, HEAD_DIM),
        preferred_element_type=jnp.float32,
    )
    masked = jnp.where(allowed[None], scores * (1.0 / math.sqrt(HEAD_DIM)), NEG)
    weight = jnp.exp(masked - jnp.max(masked, axis=2, keepdims=True))
    total = jnp.sum(weight, axis=2)
    summed = jnp.einsum(
        "hqk,khd->hqd",
        weight.astype(jnp.bfloat16),
        piece[1].reshape(count, heads_here, HEAD_DIM),
        preferred_element_type=jnp.float32,
    )
    return (summed / total[..., None]).transpose(1, 0, 2).reshape(rows, width).astype(jnp.bfloat16)


def send(value, pairs):
    return lax.ppermute(value, "ctx", pairs)


def shift(value, steps):
    count = lax.axis_size("ctx")
    return send(value, [(i, i + steps) for i in range(count) if 0 <= i + steps < count])


def in_pairs(ctx, width):
    count = width // HEAD_DIM
    return ctx == 4 and count % 2 == 0 and count // 2 <= SLOT


def in_turn(streams, short_filter, decay_rate, residue, skip_gain, lengths, queries, keys):
    f32, bf16 = jnp.float32, jnp.bfloat16
    shape = jax.ShapeDtypeStruct
    rows, width = streams.shape[1:]
    half = width // 2
    modes = decay_rate.shape[1]
    tiles = width // LANES
    ctx = lax.axis_size("ctx")
    halves = shape((rows, half), bf16)
    states = (modes * tiles, LANES)
    carried = ((modes + 3 * (SHORT - 1)) * tiles, LANES)

    given = (streams, short_filter, decay_rate.T, residue.T, skip_gain.reshape(tiles, LANES))
    q_near, q_far, k_near, k_far, *given = call(
        pack, (halves,) * 4 + tuple(shape(a.shape, a.dtype) for a in given), 2 + len(given), 0,
        scratch=[pltpu.SemaphoreType.DMA((4 + len(given),))], space=HBM,
    )(*(pltpu.with_memory_space_constraint(a, pltpu.HBM) for a in (queries, keys, *given)))
    q2 = send(q_far, [(3, 1)])
    q1 = shift(q_near, -1)
    k1 = shift(k_near, 1)
    k2 = send(k_far, [(0, 2)])

    carry, nears, others = (), [], []
    for me in range(ctx):
        last = me == ctx - 1
        near, other, *after = call(
            functools.partial(stage, me, last),
            (halves, halves) + (() if last else (shape(carried, bf16),)),
            6 + len(carry),
            scratch=[
                pltpu.VMEM((rows, width), f32),
                pltpu.VMEM((rows * tiles, LANES), f32),
                pltpu.VMEM((rows * tiles, LANES), f32),
                pltpu.VMEM(states, f32),
                pltpu.VMEM(states, f32),
                pltpu.VMEM(carried, f32),
                pltpu.VMEM((2, 3, SHORT - 1, rows + 16, LANES), f32),
            ],
        )(lengths, *given, *carry)
        carry = [send(a, [(me, me + 1)]) for a in after]
        nears.append(near)
        others.append(other)
    va = send(nears[0], [(0, 1)])
    v2 = send(others[0], [(0, 2)])
    vb = send(nears[1], [(1, 2)])
    vc = send(nears[2], [(2, 3)])

    wide = shape((rows, half + LANES), bf16)
    o_far = call(hub_far, wide, 6)(lengths, q2, keys, others[1], k1, va)
    far = send(o_far, [(1, 3)])
    o_mid = call(hub_mid, wide, 7)(
        lengths, q1, keys, others[0], others[1], k1, va
    )
    near_a = send(o_mid, [(0, 1), (1, 2)])
    o_last = call(hub_last, wide, 8)(
        lengths, q1, keys, others[2], k1, vb, k2, v2
    )
    near_b = send(o_last, [(2, 3)])
    means = (shape((rows, width), f32), shape((rows, 2 * LANES), f32))
    early = call(own_early, means, 10)(lengths, queries, keys, k1, va, *nears[:3], *others[:2])
    value, *late = call(
        own_late, (shape((rows, width), bf16), *means), 8 + 2 * ctx
    )(lengths, queries, keys, k1, vb, vc, k2, v2, *nears, *others)
    attended = call(merge, shape((rows, width), bf16), 7, 0)(*early, *late, near_a, near_b, far)
    return value, attended


def gathered(streams, short_filter, decay_rate, residue, skip_gain, lengths, queries, keys):
    f32, bf16 = jnp.float32, jnp.bfloat16
    shape = jax.ShapeDtypeStruct
    rows, width = streams.shape[1:]
    modes = decay_rate.shape[1]
    tiles = width // LANES
    ctx = lax.axis_size("ctx")
    rim = shift(streams[:, rows - SHORT + 1 :, :], 1)
    states = (modes * tiles, LANES)
    gate, long, state, step, block = call(
        hyena_local,
        (
            shape((rows, width), f32),
            shape((rows * tiles, LANES), f32),
            shape(states, bf16),
            shape(states, f32),
            shape(states, f32),
        ),
        7,
        scratch=[
            pltpu.VMEM((rows * tiles, LANES), f32),
            pltpu.VMEM(states, f32),
            pltpu.VMEM(states, f32),
        ],
    )(lengths, streams, rim, short_filter, decay_rate.T, residue.T, skip_gain.reshape(tiles, LANES))
    every = lax.all_gather(state, "ctx").astype(f32)
    ends = jnp.cumsum(lengths)
    before = lax.axis_index("ctx") * rows - 1
    lasts = (jnp.arange(ctx, dtype=jnp.int32) + 1) * rows - 1
    same = (lasts <= before) & (doc_of(lasts, ends) == doc_of(jnp.reshape(before, (1,)), ends))
    factor = jnp.where(same, (before - lasts) // rows, 0).astype(f32)
    weight = same.astype(f32)[:, None, None] * block[None] ** factor[:, None, None]
    value = call(
        functools.partial(hyena_cross, (0,)),
        shape((rows, width), bf16),
        6,
        scratch=[pltpu.VMEM((rows * tiles, LANES), f32)],
    )(lengths, step, block, long, gate, jnp.sum(weight * every, axis=0))
    return value, gathered_attention(lengths, queries, keys, value)


def shards(streams, *rest):
    plan = in_turn if in_pairs(lax.axis_size("ctx"), streams.shape[2]) else gathered
    return plan(streams, *rest)


def solution(mesh):
    placed = (
        P(None, ("groups", "ctx"), "tp"),
        P(None, None, "tp"),
        P("tp", None),
        P("tp", None),
        P("tp"),
        P("groups"),
        P(("groups", "ctx"), "tp"),
        P(("groups", "ctx"), "tp"),
    )

    return jax.shard_map(
        shards,
        mesh=mesh,
        in_specs=placed,
        out_specs=(P(("groups", "ctx"), "tp"), P(("groups", "ctx"), "tp")),
        check_vma=False,
    )
```

```python
import functools
import math

import jax
import jax.numpy as jnp
from jax import lax
from jax.experimental import pallas as pl
from jax.experimental.pallas import tpu as pltpu
from jax.sharding import PartitionSpec as P


HEAD_DIM = 128
SHORT = 3
LANES = 128
NEG = -1e30


SMEM = pl.BlockSpec(memory_space=pltpu.SMEM)
VMEM = pl.BlockSpec(memory_space=pltpu.VMEM)
HBM = pl.BlockSpec(memory_space=pltpu.HBM)
SLOT = 32


def ends_of(lengths_ref):
    ends, total = [], jnp.int32(0)
    for r in range(lengths_ref.shape[0]):
        total = total + lengths_ref[r]
        ends.append(total)
    return ends


def start_of(place, ends):
    start = jnp.zeros_like(place)
    for end in ends:
        start = jnp.where(place >= end, end, start)
    return start


def end_of(place, ends):
    stop = ends[-1]
    for end in reversed(ends):
        stop = jnp.where(place < end, end, stop)
    return stop


def call(body, out, n_in, n_smem=1, scratch=(), flops=10**7, moved=4 * 10**6, space=VMEM,
         aliases=None):
    return pl.pallas_call(
        body,
        out_shape=out,
        in_specs=[SMEM] * n_smem + [space] * (n_in - n_smem),
        out_specs=jax.tree.map(lambda _: VMEM, out),
        scratch_shapes=list(scratch),
        compiler_params=pltpu.CompilerParams(vmem_limit_bytes=16 << 20),
        input_output_aliases=aliases or {},
        cost_estimate=pl.CostEstimate(flops=flops, bytes_accessed=moved, transcendentals=0),
    )


def hyena_local(lengths_ref, streams_ref, rim_ref, taps_ref, decay_ref, residue_ref, skip_ref,
                gate_ref, long_ref, state_ref, step_ref, block_ref,
                mixed_ref, gain_ref, final_ref):
    rows, width = gate_ref.shape
    modes = decay_ref.shape[0]
    tiles = width // LANES
    index = lax.axis_index("ctx")
    first = index * rows
    ends = ends_of(lengths_ref)

    row = lax.broadcasted_iota(jnp.int32, (rows, LANES), 0)
    place = row + first
    start = start_of(place, ends)
    inside = [None] + [(place - i >= start).astype(jnp.float32) for i in range(1, SHORT)]

    for j in range(tiles):
        lanes = slice(j * LANES, (j + 1) * LANES)
        filtered = []
        for s in range(3):
            x = streams_ref[s, :, lanes].astype(jnp.float32)
            rim = rim_ref[s, :, lanes].astype(jnp.float32)
            total = taps_ref[0, s : s + 1, lanes] * x
            for i in range(1, SHORT):
                moved = pltpu.roll(x, i, 0)
                for k in range(i):
                    moved = jnp.where(row == k, rim[SHORT - 1 - i + k : SHORT - i + k, :], moved)
                total = total + taps_ref[i, s : s + 1, lanes] * moved * inside[i]
            filtered.append(total)
        gate_ref[:, lanes] = filtered[0]
        mixed_ref[pl.ds(j, rows, stride=tiles), :] = filtered[1] * filtered[2]
        rate = decay_ref[:, lanes]
        step_ref[pl.ds(j, modes, stride=tiles), :] = jnp.exp(-rate)
        block_ref[pl.ds(j, modes, stride=tiles), :] = jnp.exp(-rate * rows)
        gain_ref[pl.ds(j, modes, stride=tiles), :] = residue_ref[:, lanes]

    for h in range(tiles // 8):
        decay = [step_ref[m * tiles + h * 8 : m * tiles + h * 8 + 8, :] for m in range(modes)]
        gain = [gain_ref[m * tiles + h * 8 : m * tiles + h * 8 + 8, :] for m in range(modes)]
        skip = skip_ref[h * 8 : h * 8 + 8, :]

        def advance(t, state):
            at = pl.ds(pl.multiple_of(t * tiles + h * 8, 8), 8)
            x = mixed_ref[at, :]
            state = tuple(s * d + g * x for s, d, g in zip(state, decay, gain))
            terms = list(state) + [skip * x]
            while len(terms) > 1:
                terms = [a + b for a, b in zip(terms[::2], terms[1::2])] + (
                    [terms[-1]] if len(terms) % 2 else []
                )
            long_ref[at, :] = terms[0]
            return state

        low = jnp.int32(0)
        for end in ends:
            high = jnp.clip(end - first, 0, rows)
            low_row = low

            def four(g, state, low_row=low_row):
                for u in range(4):
                    state = advance(low_row + g * 4 + u, state)
                return state

            groups = lax.shift_right_logical(high - low_row, 2)
            state = tuple(jnp.zeros((8, LANES), jnp.float32) for _ in range(modes))
            state = lax.fori_loop(0, groups, four, state)
            state = lax.fori_loop(low_row + groups * 4, high, advance, state)

            @pl.when((low_row < high) & (high == rows))
            def _(state=state):
                for m in range(modes):
                    final_ref[m * tiles + h * 8 : m * tiles + h * 8 + 8, :] = state[m]

            low = high
    state_ref[...] = final_ref[...].astype(state_ref.dtype)


def hyena_cross(hops, lengths_ref, step_ref, block_ref, long_ref, gate_ref, *refs):
    parts = refs[: len(hops)]
    value_ref, cross_ref = refs[len(hops) :]
    rows, width = gate_ref.shape
    tiles = width // LANES
    modes = step_ref.shape[0] // tiles
    index = lax.axis_index("ctx")
    first = index * rows
    ends = ends_of(lengths_ref)
    start = start_of(first - 1, ends)
    count = jnp.where(index > 0, jnp.clip(end_of(first - 1, ends) - first, 0, rows), 0)
    keeps = [
        ((first - 1 - hop * rows >= start) & (index > hop)).astype(jnp.float32) for hop in hops
    ]

    @pl.when(count > 0)
    def _():
        for h in range(tiles // 8):
            decay, incoming = [], []
            for m in range(modes):
                at = slice(m * tiles + h * 8, m * tiles + h * 8 + 8)
                decay.append(step_ref[at, :])
                total, factor = None, None
                for hop, keep, part in zip(hops, keeps, parts):
                    term = part[at, :].astype(jnp.float32) * keep
                    if hop:
                        factor = block_ref[at, :] if factor is None else factor * block_ref[at, :]
                        term = term * factor
                    total = term if total is None else total + term
                incoming.append(total)

            def advance(t, state):
                at = pl.ds(pl.multiple_of(t * tiles + h * 8, 8), 8)
                state = tuple(s * d for s, d in zip(state, decay))
                terms = list(state)
                while len(terms) > 1:
                    terms = [a + b for a, b in zip(terms[::2], terms[1::2])] + (
                        [terms[-1]] if len(terms) % 2 else []
                    )
                cross_ref[at, :] = terms[0]
                return state

            def four(g, state):
                for u in range(4):
                    state = advance(g * 4 + u, state)
                return state

            groups = lax.shift_right_logical(count, 2)
            state = lax.fori_loop(0, groups, four, tuple(incoming))
            lax.fori_loop(groups * 4, count, advance, state)

    row = lax.broadcasted_iota(jnp.int32, (rows, LANES), 0)
    reached = row < count
    for j in range(tiles):
        lanes = slice(j * LANES, (j + 1) * LANES)
        every = pl.ds(j, rows, stride=tiles)
        long = long_ref[every, :] + jnp.where(reached, cross_ref[every, :], 0.0)
        value_ref[:, lanes] = (gate_ref[:, lanes] * long).astype(value_ref.dtype)


def tree_sum(terms):
    while len(terms) > 1:
        odd = [terms[-1]] if len(terms) % 2 else []
        terms = [a + b for a, b in zip(terms[::2], terms[1::2])] + odd
    return terms[0]


EDGE = SHORT - 1


def prepare(lengths_ref, streams_ref, taps_ref, decay_ref, residue_ref,
            gate_ref, mixed_ref, step_ref, gain_ref, edge_ref, shifted_ref):
    rows, width = gate_ref.shape
    modes = decay_ref.shape[0]
    tiles = width // LANES
    first = lax.axis_index("ctx") * rows
    ends = ends_of(lengths_ref)
    zero = jnp.zeros((8, LANES), jnp.float32)
    for j in range(tiles):
        lanes = slice(j * LANES, (j + 1) * LANES)

        def keep(kind, s, k, value):
            at = ((kind * 3 + s) * EDGE + k) * tiles + j
            edge_ref[at : at + 1, :] = value

        filtered = []
        for s in range(3):
            x = streams_ref[s, :, lanes].astype(jnp.float32)
            total = taps_ref[0, s : s + 1, lanes] * x
            for i in range(1, SHORT):
                buffer = shifted_ref.at[j % 2, s, i - 1]
                buffer[:8, :] = zero
                buffer[8 : 8 + rows, :] = x
                for end in ends[:-1]:
                    inside = (end > first) & (end < first + rows)
                    for k in range(1, i + 1):
                        at = jnp.where(inside, 8 + end - first - k, rows + 8)
                        buffer[pl.ds(at, 1), :] = zero[:1]
                total = total + taps_ref[i, s : s + 1, lanes] * buffer[8 - i : 8 - i + rows, :]
                keep(2, s, i - 1, taps_ref[i, s : s + 1, lanes])
            filtered.append(total)
            for k in range(EDGE):
                keep(0, s, k, x[rows - EDGE + k : rows - EDGE + k + 1, :])
                keep(1, s, k, total[k : k + 1, :])
        gate_ref[:, lanes] = filtered[0]
        mixed_ref[pl.ds(j, rows, stride=tiles), :] = filtered[1] * filtered[2]
        step_ref[pl.ds(j, modes, stride=tiles), :] = jnp.exp(-decay_ref[:, lanes])
        gain_ref[pl.ds(j, modes, stride=tiles), :] = residue_ref[:, lanes]


def stage(me, last, lengths_ref, given_ref, gate_ref, step_ref, gain_ref, edge_ref, skip_ref, *refs):
    refs = list(refs)
    carry_ref = refs.pop(0) if me else None
    near_ref, other_ref = refs[:2]
    next_ref = None if last else refs[2]
    mixed_ref = refs[-3] if me else given_ref
    long_ref, carried_ref = refs[-2:]
    rows, half = near_ref.shape
    width = 2 * half
    tiles = width // LANES
    states = step_ref.shape[0]
    modes = states // tiles
    first = me * rows

    def edge(kind, s, k):
        at = ((kind * 3 + s) * EDGE + k) * tiles
        return edge_ref[at : at + tiles, :]

    def run():
        ends = ends_of(lengths_ref)
        starts = [start_of(jnp.int32(first + k), ends) for k in range(EDGE)]
        goes_on = (starts[0] <= first - 1).astype(jnp.float32)
        late = [None] * EDGE
        if me:
            carried_ref[...] = carry_ref[...].astype(jnp.float32)
            firsts = []
            for s in range(3):
                adds = []
                for k in range(EDGE):
                    total = jnp.zeros((tiles, LANES), jnp.float32)
                    for i in range(k + 1, SHORT):
                        at = states + (s * EDGE + EDGE + k - i) * tiles
                        same = (starts[k] <= first + k - i).astype(jnp.float32)
                        total = total + edge(2, s, i - 1) * carried_ref[at : at + tiles, :] * same
                    adds.append(total)
                firsts.append(adds)
            late = firsts[0]
            for k in range(EDGE):
                mixed_ref[k * tiles : (k + 1) * tiles, :] = (edge(1, 1, k) + firsts[1][k]) * (
                    edge(1, 2, k) + firsts[2][k]
                )

        for h in range(tiles // 8):
            spots = [slice(m * tiles + h * 8, m * tiles + h * 8 + 8) for m in range(modes)]
            decay = [step_ref[at, :] for at in spots]
            gain = [gain_ref[at, :] for at in spots]
            skip = skip_ref[h * 8 : h * 8 + 8, :]

            def advance(t, state):
                at = pl.ds(pl.multiple_of(t * tiles + h * 8, 8), 8)
                x = mixed_ref[at, :]
                state = tuple(s * d + g * x for s, d, g in zip(state, decay, gain))
                long_ref[at, :] = tree_sum(list(state) + [skip * x])
                return state

            incoming = [carried_ref[at, :] * goes_on for at in spots] if me else None
            low = jnp.int32(0)
            for end in ends:
                high = jnp.clip(end - first, 0, rows)

                def four(g, state, low=low):
                    for u in range(4):
                        state = advance(low + g * 4 + u, state)
                    return state

                groups = lax.shift_right_logical(high - low, 2)
                if me:
                    at_start = (low == 0).astype(jnp.float32)
                    state = tuple(s * at_start for s in incoming)
                else:
                    state = tuple(jnp.zeros((8, LANES), jnp.float32) for _ in spots)
                state = lax.fori_loop(0, groups, four, state)
                state = lax.fori_loop(low + groups * 4, high, advance, state)
                if not last:

                    @pl.when((low < high) & (high == rows))
                    def _(state=state):
                        for at, s in zip(spots, state):
                            carried_ref[at, :] = s

                low = high
        if not last:
            carried_ref[states:, :] = edge_ref[: 3 * EDGE * tiles, :]
            next_ref[...] = carried_ref[...].astype(next_ref.dtype)
        lower, upper = (near_ref, other_ref) if me % 2 else (other_ref, near_ref)
        row = lax.broadcasted_iota(jnp.int32, (8, LANES), 0)
        for j in range(tiles):
            long = long_ref[pl.ds(j, rows, stride=tiles), :]
            gate = gate_ref[:, j * LANES : (j + 1) * LANES]
            if me:
                top = gate[:8]
                for k in range(EDGE):
                    top = top + jnp.where(row == k, late[k][j : j + 1, :], 0.0)
                gate = jnp.concatenate([top, gate[8:]], axis=0)
            out, at = (lower, j) if j < tiles // 2 else (upper, j - tiles // 2)
            out[:, at * LANES : (at + 1) * LANES] = (gate * long).astype(out.dtype)

    pl.when(lax.axis_index("ctx") == me)(run)


def pack(queries_ref, keys_ref, *refs):
    count = (len(refs) - 5) // 2
    given, (q_near, q_far, k_near, k_far), held = refs[:count], refs[count:][:4], refs[count + 4 : -1]
    sems = refs[-1]
    half = q_far.shape[1]
    even = 1 - lax.axis_index("ctx") % 2
    near = pl.ds(pl.multiple_of(even * half, half), half)
    copies = [
        pltpu.make_async_copy(source, target, sems.at[i])
        for i, (source, target) in enumerate((
            *zip(given, held),
            (queries_ref.at[:, half:], q_far),
            (keys_ref.at[:, near], k_near),
            (keys_ref.at[:, :half], k_far),
            (queries_ref.at[:, near], q_near),
        ))
    ]
    for copy in copies:
        copy.start()
    for copy in copies:
        copy.wait()


def biases(query_block, key_blocks, rows, ends):
    place = query_block * rows + lax.broadcasted_iota(jnp.int32, (rows, rows), 0)
    start = start_of(place, ends)
    out = []
    for block in key_blocks:
        key = block * rows + lax.broadcasted_iota(jnp.int32, (rows, rows), 1)
        out.append(jnp.where((key >= start) & (key <= place), 0.0, NEG))
    return out


def one_head(query, keys, values, bias):
    scale = 1.0 / math.sqrt(HEAD_DIM)
    base2 = scale * math.log2(math.e)
    key = keys[0] if len(keys) == 1 else jnp.concatenate(keys, axis=0)
    value = values[0] if len(values) == 1 else jnp.concatenate(values, axis=0)
    scores = lax.dot_general(
        query, key, (((1,), (1,)), ((), ())), preferred_element_type=jnp.float32
    ) + bias
    top = jnp.max(scores, axis=1, keepdims=True)
    weights = jnp.exp2((scores - top) * base2)
    total = jnp.sum(weights, axis=1, keepdims=True)
    summed = jnp.dot(weights.astype(jnp.bfloat16), value, preferred_element_type=jnp.float32)
    return summed / total, top * scale + jnp.log(total)


def cut(ref, h):
    return ref[:, h * HEAD_DIM : (h + 1) * HEAD_DIM]


def split3(x):
    a = x.astype(jnp.bfloat16)
    rest = x - a.astype(jnp.float32)
    b = rest.astype(jnp.bfloat16)
    c = (rest - b.astype(jnp.float32)).astype(jnp.bfloat16)
    return a, b, c


def attend(query_block, query_ref, query_at, sources, rows, count, ends, write):
    bias = jnp.concatenate(
        biases(query_block, [block for block, _, _, _ in sources], rows, ends), axis=1
    )
    for h in range(count):
        held_keys = [cut(keys, at + h) for _, keys, at, _ in sources]
        held_values = [cut(values, h) for _, _, _, values in sources]
        write(h, *one_head(cut(query_ref, query_at + h), held_keys, held_values, bias))


def serve(query_block, query_ref, sources, ends, out_ref):
    rows, half = query_ref.shape
    lane = lax.broadcasted_iota(jnp.int32, (rows, LANES), 1)
    stats = [jnp.zeros((rows, LANES), jnp.float32)]

    def write(h, mean, log_total):
        out_ref[:, h * HEAD_DIM : (h + 1) * HEAD_DIM] = mean.astype(out_ref.dtype)
        for k, piece in enumerate(split3(log_total)):
            stats[0] = jnp.where(lane == SLOT * k + h, piece.astype(jnp.float32), stats[0])

    attend(query_block, query_ref, 0, sources, rows, half // HEAD_DIM, ends, write)
    out_ref[:, half:] = stats[0].astype(out_ref.dtype)


def hub_far(lengths_ref, q2_ref, key_ref, other_ref, k1_ref, va_ref, far_ref):
    count = q2_ref.shape[1] // HEAD_DIM

    @pl.when(lax.axis_index("ctx") == 1)
    def _():
        sources = [(1, key_ref, count, other_ref), (0, k1_ref, 0, va_ref)]
        serve(3, q2_ref, sources, ends_of(lengths_ref), far_ref)


def hub_mid(lengths_ref, q1_ref, key_ref, other0, other1, k1_ref, va_ref, near_ref):
    count = q1_ref.shape[1] // HEAD_DIM
    index = lax.axis_index("ctx")
    ends = ends_of(lengths_ref)

    @pl.when(index == 0)
    def _():
        serve(1, q1_ref, [(0, key_ref, 0, other0)], ends, near_ref)

    @pl.when(index == 1)
    def _():
        sources = [(1, key_ref, count, other1), (0, k1_ref, 0, va_ref)]
        serve(2, q1_ref, sources, ends, near_ref)


def hub_last(lengths_ref, q1_ref, key_ref, other_ref, k1_ref, vb_ref, k2_ref, v2_ref, near_ref):
    @pl.when(lax.axis_index("ctx") == 2)
    def _():
        sources = [(2, key_ref, 0, other_ref), (1, k1_ref, 0, vb_ref), (0, k2_ref, 0, v2_ref)]
        serve(3, q1_ref, sources, ends_of(lengths_ref), near_ref)


def own_half(query_ref, key_ref, mean_ref, stat_ref, ends, base, values, more=()):
    rows, width = query_ref.shape
    index = lax.axis_index("ctx")
    lane = lax.broadcasted_iota(jnp.int32, (rows, LANES), 1)
    stats = [jnp.zeros((rows, LANES), jnp.float32)]

    def write(h, mean, log_total):
        mean_ref[:, (base + h) * HEAD_DIM : (base + h + 1) * HEAD_DIM] = mean
        stats[0] = jnp.where(lane == h, log_total, stats[0])

    sources = [(index, key_ref, base, values), *more]
    attend(index, query_ref, base, sources, rows, width // HEAD_DIM // 2, ends, write)
    stat_ref[:, (LANES if base else 0) : (2 * LANES if base else LANES)] = stats[0]


def own_early(lengths_ref, query_ref, key_ref, k1_ref, va_ref, near0, near1, near2, other0, other1,
              mean_ref, stat_ref):
    count = query_ref.shape[1] // HEAD_DIM // 2
    index = lax.axis_index("ctx")
    run = functools.partial(
        own_half, query_ref, key_ref, mean_ref, stat_ref, ends_of(lengths_ref)
    )

    @pl.when(index == 0)
    def _():
        run(0, other0)
        run(count, near0)

    @pl.when(index == 1)
    def _():
        run(0, near1)
        run(count, other1, [(0, k1_ref, 0, va_ref)])

    @pl.when(index == 2)
    def _():
        run(count, near2)


def own_late(lengths_ref, query_ref, key_ref, k1_ref, vb_ref, vc_ref, k2_ref, v2_ref,
             near0, near1, near2, near3, other0, other1, other2, other3,
             value_ref, mean_ref, stat_ref):
    count = query_ref.shape[1] // HEAD_DIM // 2
    half = near0.shape[1]
    index = lax.axis_index("ctx")
    run = functools.partial(
        own_half, query_ref, key_ref, mean_ref, stat_ref, ends_of(lengths_ref)
    )
    for me, (lower, upper) in enumerate(
        ((other0, near0), (near1, other1), (other2, near2), (near3, other3))
    ):
        @pl.when(index == me)
        def _(lower=lower, upper=upper):
            value_ref[:, :half] = lower[...]
            value_ref[:, half:] = upper[...]

    @pl.when(index == 2)
    def _():
        run(0, other2, [(1, k1_ref, 0, vb_ref), (0, k2_ref, 0, v2_ref)])

    @pl.when(index == 3)
    def _():
        run(0, near3)
        run(count, other3, [(2, k1_ref, 0, vc_ref)])


def merge(early_ref, early_stat, late_ref, late_stat, near_a, near_b, far_ref, out_ref):
    _, width = early_ref.shape
    half = width // 2
    count = half // HEAD_DIM
    index = lax.axis_index("ctx")

    def join(base, mean_ref, stat_ref, other_ref):
        here = stat_ref[:, (LANES if base else 0) : (2 * LANES if base else LANES)]
        there = other_ref[:, half:].astype(jnp.float32)
        there = there + pltpu.roll(there, LANES - SLOT, 1) + pltpu.roll(there, LANES - 2 * SLOT, 1)
        top = jnp.maximum(here, there)
        a, b = jnp.exp(here - top), jnp.exp(there - top)
        norm = 1.0 / (a + b)
        a, b = a * norm, b * norm
        for h in range(count):
            at = slice((h + base) * HEAD_DIM, (h + base + 1) * HEAD_DIM)
            other = cut(other_ref, h).astype(jnp.float32)
            out_ref[:, at] = (
                mean_ref[:, at] * a[:, h : h + 1] + other * b[:, h : h + 1]
            ).astype(out_ref.dtype)

    def keep(base, mean_ref):
        at = slice(base * HEAD_DIM, (base + count) * HEAD_DIM)
        out_ref[:, at] = mean_ref[:, at].astype(out_ref.dtype)

    @pl.when(index == 0)
    def _():
        keep(0, early_ref)
        keep(count, early_ref)

    @pl.when(index == 1)
    def _():
        join(0, early_ref, early_stat, near_a)
        keep(count, early_ref)

    @pl.when(index == 2)
    def _():
        keep(0, late_ref)
        join(count, early_ref, early_stat, near_a)

    @pl.when(index == 3)
    def _():
        join(0, late_ref, late_stat, near_b)
        join(count, late_ref, late_stat, far_ref)


def doc_of(places, ends):
    return jnp.sum((places[:, None] >= ends[None, :]).astype(jnp.int32), axis=1)


def gathered_attention(lengths, queries, keys, values):
    rows, width = queries.shape
    heads_here = width // HEAD_DIM
    ends = jnp.cumsum(lengths)
    places = lax.axis_index("ctx") * rows + jnp.arange(rows, dtype=jnp.int32)
    piece = lax.all_gather(jnp.stack([keys, values]), "ctx", axis=1, tiled=True)
    count = piece.shape[1]
    key_places = jnp.arange(count, dtype=jnp.int32)
    allowed = (key_places[None, :] <= places[:, None]) & (
        doc_of(key_places, ends)[None, :] == doc_of(places, ends)[:, None]
    )
    scores = jnp.einsum(
        "qhd,khd->hqk",
        queries.reshape(rows, heads_here, HEAD_DIM),
        piece[0].reshape(count, heads_here, HEAD_DIM),
        preferred_element_type=jnp.float32,
    )
    masked = jnp.where(allowed[None], scores * (1.0 / math.sqrt(HEAD_DIM)), NEG)
    weight = jnp.exp(masked - jnp.max(masked, axis=2, keepdims=True))
    total = jnp.sum(weight, axis=2)
    summed = jnp.einsum(
        "hqk,khd->hqd",
        weight.astype(jnp.bfloat16),
        piece[1].reshape(count, heads_here, HEAD_DIM),
        preferred_element_type=jnp.float32,
    )
    return (summed / total[..., None]).transpose(1, 0, 2).reshape(rows, width).astype(jnp.bfloat16)


def send(value, pairs):
    return lax.ppermute(value, "ctx", pairs)


def shift(value, steps):
    count = lax.axis_size("ctx")
    return send(value, [(i, i + steps) for i in range(count) if 0 <= i + steps < count])


def in_pairs(ctx, width):
    count = width // HEAD_DIM
    return ctx == 4 and count % 2 == 0 and count // 2 <= SLOT


def in_turn(streams, short_filter, decay_rate, residue, skip_gain, lengths, queries, keys):
    f32, bf16 = jnp.float32, jnp.bfloat16
    shape = jax.ShapeDtypeStruct
    rows, width = streams.shape[1:]
    half = width // 2
    modes = decay_rate.shape[1]
    tiles = width // LANES
    ctx = lax.axis_size("ctx")
    halves = shape((rows, half), bf16)
    states = (modes * tiles, LANES)
    carried = ((modes + 3 * (SHORT - 1)) * tiles, LANES)

    given = (streams, short_filter, decay_rate.T, residue.T, skip_gain.reshape(tiles, LANES))
    q_near, q_far, k_near, k_far, *given = call(
        pack, (halves,) * 4 + tuple(shape(a.shape, a.dtype) for a in given), 2 + len(given), 0,
        scratch=[pltpu.SemaphoreType.DMA((4 + len(given),))], space=HBM,
    )(*(pltpu.with_memory_space_constraint(a, pltpu.HBM) for a in (queries, keys, *given)))
    q2 = send(q_far, [(3, 1)])
    q1 = shift(q_near, -1)
    k1 = shift(k_near, 1)
    k2 = send(k_far, [(0, 2)])

    long = shape((rows * tiles, LANES), f32)
    gate, mixed, step, gain, edge = call(
        prepare,
        (
            shape((rows, width), f32),
            long,
            shape(states, f32),
            shape(states, f32),
            shape((9 * EDGE * tiles, LANES), f32),
        ),
        5,
        scratch=[pltpu.VMEM((2, 3, EDGE, rows + 16, LANES), f32)],
    )(lengths, *given[:-1])
    carry, nears, others = (), [], []
    for me in range(ctx):
        last = me == ctx - 1
        near, other, *after = call(
            functools.partial(stage, me, last),
            (halves, halves)
            + (() if last else (shape(carried, bf16),))
            + ((long,) if me else ()),
            7 + len(carry),
            scratch=[pltpu.VMEM((rows * tiles, LANES), f32), pltpu.VMEM(carried, f32)],
            aliases={1: 2 if last else 3} if me else None,
        )(lengths, mixed, gate, step, gain, edge, given[-1], *carry)
        if me:
            mixed = after.pop()
        carry = [send(a, [(me, me + 1)]) for a in after]
        nears.append(near)
        others.append(other)
    va = send(nears[0], [(0, 1)])
    v2 = send(others[0], [(0, 2)])
    vb = send(nears[1], [(1, 2)])
    vc = send(nears[2], [(2, 3)])

    wide = shape((rows, half + LANES), bf16)
    o_far = call(hub_far, wide, 6)(lengths, q2, keys, others[1], k1, va)
    far = send(o_far, [(1, 3)])
    o_mid = call(hub_mid, wide, 7)(
        lengths, q1, keys, others[0], others[1], k1, va
    )
    near_a = send(o_mid, [(0, 1), (1, 2)])
    o_last = call(hub_last, wide, 8)(
        lengths, q1, keys, others[2], k1, vb, k2, v2
    )
    near_b = send(o_last, [(2, 3)])
    means = (shape((rows, width), f32), shape((rows, 2 * LANES), f32))
    early = call(own_early, means, 10)(lengths, queries, keys, k1, va, *nears[:3], *others[:2])
    value, *late = call(
        own_late, (shape((rows, width), bf16), *means), 8 + 2 * ctx
    )(lengths, queries, keys, k1, vb, vc, k2, v2, *nears, *others)
    attended = call(merge, shape((rows, width), bf16), 7, 0)(*early, *late, near_a, near_b, far)
    return value, attended


def gathered(streams, short_filter, decay_rate, residue, skip_gain, lengths, queries, keys):
    f32, bf16 = jnp.float32, jnp.bfloat16
    shape = jax.ShapeDtypeStruct
    rows, width = streams.shape[1:]
    modes = decay_rate.shape[1]
    tiles = width // LANES
    ctx = lax.axis_size("ctx")
    rim = shift(streams[:, rows - SHORT + 1 :, :], 1)
    states = (modes * tiles, LANES)
    gate, long, state, step, block = call(
        hyena_local,
        (
            shape((rows, width), f32),
            shape((rows * tiles, LANES), f32),
            shape(states, bf16),
            shape(states, f32),
            shape(states, f32),
        ),
        7,
        scratch=[
            pltpu.VMEM((rows * tiles, LANES), f32),
            pltpu.VMEM(states, f32),
            pltpu.VMEM(states, f32),
        ],
    )(lengths, streams, rim, short_filter, decay_rate.T, residue.T, skip_gain.reshape(tiles, LANES))
    every = lax.all_gather(state, "ctx").astype(f32)
    ends = jnp.cumsum(lengths)
    before = lax.axis_index("ctx") * rows - 1
    lasts = (jnp.arange(ctx, dtype=jnp.int32) + 1) * rows - 1
    same = (lasts <= before) & (doc_of(lasts, ends) == doc_of(jnp.reshape(before, (1,)), ends))
    factor = jnp.where(same, (before - lasts) // rows, 0).astype(f32)
    weight = same.astype(f32)[:, None, None] * block[None] ** factor[:, None, None]
    value = call(
        functools.partial(hyena_cross, (0,)),
        shape((rows, width), bf16),
        6,
        scratch=[pltpu.VMEM((rows * tiles, LANES), f32)],
    )(lengths, step, block, long, gate, jnp.sum(weight * every, axis=0))
    return value, gathered_attention(lengths, queries, keys, value)


def shards(streams, *rest):
    plan = in_turn if in_pairs(lax.axis_size("ctx"), streams.shape[2]) else gathered
    return plan(streams, *rest)


def solution(mesh):
    placed = (
        P(None, ("groups", "ctx"), "tp"),
        P(None, None, "tp"),
        P("tp", None),
        P("tp", None),
        P("tp"),
        P("groups"),
        P(("groups", "ctx"), "tp"),
        P(("groups", "ctx"), "tp"),
    )

    return jax.shard_map(
        shards,
        mesh=mesh,
        in_specs=placed,
        out_specs=(P(("groups", "ctx"), "tp"), P(("groups", "ctx"), "tp")),
        check_vma=False,
    )
```
